256 devices in a mesh: tm: 8 (over z_lo, y), space: 32 (over z_hi, x, core).
Axes of the slice: x: 4, y: 4, z: 8 (z_hi: 4, z_lo: 2; z = z_hi * 2 + z_lo), core: 2. Of those that a mesh axis runs over, the one named last changes fastest.
Arguments:
- control: float32 [256, 51200], P(('tm', 'space')), may hold values from -4 to 4
- spectrum: float32 [51200], replicated, may hold values from 0.2 to 2
- perturb: bfloat16 [16, 256, 4, 51200], P('tm', None, None, 'space'), may hold values from -0.375 to 0.375
- obs_index: int32 [16, 65536], P('tm', 'space'), may hold values from 0 to 6399
- innovation: float32 [16, 65536], P('tm', 'space'), may hold values from -10 to 10
- obs_sigma: float32 [16, 65536], P('tm', 'space'), may hold values from 0.5 to 2
- qc_class: int32 [16, 65536], P('tm', 'space'), may hold values from 0 to 2
Outputs:
- control_out: float32 [256, 51200], P(('tm', 'space'))
- cost_list: float32 [1], replicated
The draws below stay inside these ranges and needn't reach their ends.
Inputs may be any that keep to these rules, and one draw needn't show every extreme that they name: `obs_index`: observation o of block o // 2048 observes the cell level * 1600 + point, the point counted within the block's piece of the grid; repeats may occur.
All inputs are finite; a program needn't handle non-finite values.
Results may differ from the reference program's by a relative error of at most 0.0034.
Values may be sent and summed in bfloat16 or wider, within the bound.
No kernel may reach another device: no remote copies, remote signals or barrier semaphores. Data moves between devices by JAX's collectives and lax.ppermute only.
A program may use at most 128 MiB of HBM per device.

```python
import math
import jax
import jax.numpy as jnp
from jax import lax

GX = 320
GY = 160
LEV = 4
ITERS = 1
OBS_DEV = 2048
TIMES = 16
MEMBERS = 256
NOBS = 65536
N_SPACE = 32


def set_ends(entries, stream_key, smallest, top_value):
    longest = entries.shape.index(max(entries.shape))
    spots = []
    for shift in (0, 1):
        where = [jax.random.randint(jax.random.fold_in(stream_key, axis), (), 0, length) for axis, length in enumerate(entries.shape)]
        where[longest] = (where[longest] + shift) % entries.shape[longest]
        spots.append(tuple(where))
    return entries.at[spots[0]].set(smallest).at[spots[1]].set(top_value)


def shard_levels(own_key, dims, shards, low, high):
    def one(position, shards_of):
        draws = jax.random.uniform(jax.random.fold_in(jax.random.fold_in(own_key, 6), position), (shards_of,), jnp.float32, low / len(shards), high / len(shards))
        return jnp.repeat(jnp.exp(draws), dims[position] // shards_of).reshape((-1,) + (1,) * (len(dims) - position - 1))

    factor_of = one(*shards[0])
    for cut in shards[1:]:
        factor_of = factor_of * one(*cut)
    return factor_of


def noise(key, shape, spread, most, shards=(), held_as=jnp.bfloat16):
    drawn = spread * jax.random.normal(key, shape, jnp.float32)
    if shards:
        drawn = drawn * shard_levels(key, shape, shards, -0.22, 0.18)
    return jnp.clip(drawn, -most, most).astype(held_as)


def setup_inputs(seed: int = 0) -> dict:
    key_list = jax.random.split(jax.random.key(seed), 8)
    return {
        "control": noise(key_list[0], (MEMBERS, GX * GY), 0.5, 4.0, ((0, 256),), jnp.float32),
        "spectrum": jnp.clip(jnp.exp(jax.random.uniform(key_list[1], (GX * GY,), jnp.float32, math.log(0.2), math.log(2.0))), 0.2, 2.0),
        "perturb": noise(key_list[2], (TIMES, MEMBERS, LEV, GX * GY), MEMBERS ** -0.5, 0.375, ((0, 8), (3, 32))),
        "obs_index": set_ends(jax.random.randint(key_list[3], (TIMES, NOBS), 0, LEV * (GX * GY // N_SPACE)), jax.random.fold_in(key_list[3], 1), 0, (LEV * (GX * GY // N_SPACE)) - 1).astype(jnp.int32),
        "innovation": noise(key_list[4], (TIMES, NOBS), 2.0, 10.0, ((0, 8), (1, 32)), jnp.float32),
        "obs_sigma": jnp.clip(jnp.exp(math.log(2.0) - 1.3862944 * jax.random.uniform(key_list[5], (TIMES, NOBS), jnp.float32) ** shard_levels(key_list[5], (TIMES, NOBS), ((0, 8), (1, 32)), -0.2, 0.2)), 0.5, 2.0),
        "qc_class": set_ends(jax.random.randint(key_list[6], (TIMES, NOBS), 0, 3), jax.random.fold_in(key_list[6], 1), 0, 2).astype(jnp.int32),
    }


def lookup_tables(segment_length):
    wave_num = jnp.arange(segment_length, dtype=jnp.float32)[:, None]
    grid_positions = jnp.arange(segment_length, dtype=jnp.float32)[None, :]
    basis = jnp.cos(jnp.pi * (grid_positions + 0.5) * wave_num / segment_length) * jnp.sqrt(2.0 / segment_length)
    return jnp.where(wave_num == 0, basis * jnp.sqrt(0.5), basis)

def synthesize(control, spectrum, basis_x, basis_y):
    coeffs = (control * spectrum[None, :]).reshape(control.shape[0], GX, GY)
    middle = jnp.einsum('kn,mkl->mnl', basis_x, coeffs, precision=lax.Precision.HIGHEST)
    result = jnp.einsum('mnl,lp->mnp', middle, basis_y, precision=lax.Precision.HIGHEST)
    return result.reshape(control.shape[0], GX * GY)

def analyze(adjoint, spectrum, basis_x, basis_y):
    state_fields = adjoint.reshape(adjoint.shape[0], GX, GY)
    middle = jnp.einsum('kn,mnp->mkp', basis_x, state_fields, precision=lax.Precision.HIGHEST)
    result = jnp.einsum('mkp,lp->mkl', middle, basis_y, precision=lax.Precision.HIGHEST)
    return result.reshape(adjoint.shape[0], GX * GY) * spectrum[None, :]

def reference(control, spectrum, perturb, obs_index, innovation, obs_sigma, qc_class):
    basis_x = lookup_tables(GX)
    basis_y = lookup_tables(GY)
    grid_total = GX * GY
    piece_len = grid_total // N_SPACE
    block_ids = (jnp.arange(innovation.shape[1], dtype=jnp.int32) // OBS_DEV).astype(jnp.int32)
    cell_index = obs_index // piece_len * grid_total + block_ids[None, :] * piece_len + obs_index % piece_len
    cell_index = cell_index.astype(jnp.int32)
    radius = jnp.where(qc_class == 0, 4.0, jnp.where(qc_class == 1, 2.0, 1.0)).astype(jnp.float32)
    cost_list = []

    def scatter_cells(indices, values):
        return jnp.zeros((LEV * grid_total,), jnp.float32).at[indices].add(values)
    for iteration in range(ITERS):
        member_field = synthesize(control, spectrum, basis_x, basis_y).astype(jnp.bfloat16)
        field_wide = member_field.astype(jnp.float32)

        def forward(slot_data):
            return jnp.einsum('mlg,mg->lg', slot_data.astype(jnp.float32), field_wide).reshape(-1)
        increment = lax.map(forward, perturb)
        modelled = jnp.take_along_axis(increment, cell_index, axis=1)
        scaled = (modelled - innovation) / obs_sigma
        scaled_sq = scaled * scaled / (radius * radius)
        obs_cost = jnp.sum(0.5 * radius * radius * jnp.log1p(scaled_sq))
        back_cost = 0.5 * jnp.sum(control * control)
        obs_grad = scaled / ((1.0 + scaled_sq) * obs_sigma)
        control_update = jax.vmap(scatter_cells)(cell_index, obs_grad).astype(jnp.bfloat16)

        def backward(running, pair):
            slot_data, slot_update = pair
            term = jnp.einsum('mlg,lg->mg', slot_data.astype(jnp.float32), slot_update.reshape(LEV, grid_total).astype(jnp.float32))
            return (running + term, None)
        adjoint, unused = lax.scan(backward, jnp.zeros(control.shape, jnp.float32), (perturb, control_update))
        gradient = control + analyze(adjoint, spectrum, basis_x, basis_y)
        grad_sq = jnp.sum(gradient * gradient)
        total_cost = back_cost + obs_cost
        step_size = 0.5 * total_cost / (grad_sq + 1e-06)
        control = control - step_size * gradient
        cost_list.append(total_cost)
    return (control, jnp.stack(cost_list))
```

```python
import jax
import jax.numpy as jnp
from jax import lax
from jax.experimental import pallas as pl
from jax.experimental.pallas import tpu as pltpu
from jax.sharding import Mesh
from jax.sharding import PartitionSpec as P

GX = 320
GY = 160
SPACE = ("space_0", "space_1", "space_2")
TM = ("tm_0", "tm_1")
TM_SPACE = ("tm_0", "tm_1", "space_0", "space_1", "space_2")


PIECE = 1600
LEV = 4
BLOCKS = 13
ROWS = 64
OBS = 2048
CHUNK = 256


def split3(value):
    first = value.astype(jnp.bfloat16)
    rest = value - first.astype(jnp.float32)
    second = rest.astype(jnp.bfloat16)
    third = (rest - second.astype(jnp.float32)).astype(jnp.bfloat16)
    return first, second, third


def middle_kernel(p_ref, f_ref, idx_ref, inn_ref, sig_ref, qc_ref, adj_ref, cost_ref,
                  cells, table, modelled, grads, where_row, where_lane):
    f32 = jnp.float32
    cells[...] = jnp.zeros_like(cells)

    def forward(blk, start, width):
        rows = p_ref[:, pl.ds(start, width), :].reshape(8 * width, 256)
        prod = jnp.dot(rows, f_ref[:, pl.ds(start, width)], preferred_element_type=f32)
        same = lax.broadcasted_iota(jnp.int32, (width, width), 0) == lax.broadcasted_iota(
            jnp.int32, (width, width), 1)
        for k in range(8):
            one = jnp.where(same, prod[k * width:(k + 1) * width], 0.0)
            row = jnp.sum(one, axis=0, keepdims=True)
            cells[k // LEV, pl.ds(k % LEV * BLOCKS + blk, 1), 0:width] = row

    def forward_step(blk, carry):
        forward(blk, pl.multiple_of(blk * 128, 128), 128)
        return carry

    lax.fori_loop(0, 12, forward_step, 0)
    forward(12, 1536, 64)

    index = idx_ref[...]
    level = ((index >= PIECE).astype(jnp.int32) + (index >= 2 * PIECE).astype(jnp.int32)
             + (index >= 3 * PIECE).astype(jnp.int32))
    point = index - level * PIECE
    where_row[...] = level * BLOCKS + (point >> 7)
    where_lane[...] = point & 127

    for t in range(2):
        parts = split3(jnp.transpose(cells[t]))
        for k in range(3):
            table[t, :, k * ROWS:(k + 1) * ROWS] = parts[k]

    row_id = lax.broadcasted_iota(jnp.int32, (ROWS, CHUNK), 0)
    lane_id = lax.broadcasted_iota(jnp.int32, (128, CHUNK), 0)

    for t in range(2):
        def gather_step(c, carry):
            at = pl.ds(pl.multiple_of(c * CHUNK, CHUNK), CHUNK)
            hot = jnp.where(row_id == where_row[t:t + 1, at], 1.0, 0.0).astype(jnp.bfloat16)
            hot = jnp.concatenate([hot, hot, hot], axis=0)
            lines = jnp.dot(table[t], hot, preferred_element_type=f32)
            lines = jnp.where(lane_id == where_lane[t:t + 1, at], lines, 0.0)
            modelled[t:t + 1, at] = jnp.sum(lines, axis=0, keepdims=True)
            return carry
        lax.fori_loop(0, OBS // CHUNK, gather_step, 0)

    sigma = sig_ref[...]
    kind = qc_ref[...]
    radius_sq = jnp.where(kind == 0, 16.0, jnp.where(kind == 1, 4.0, 1.0))
    scaled = (modelled[...] - inn_ref[...]) / sigma
    scaled_sq = scaled * scaled / radius_sq
    terms = 0.5 * radius_sq * jnp.log1p(scaled_sq)
    cost_ref[...] = jnp.sum(terms, axis=(0, 1), keepdims=True)
    grad = scaled / ((1.0 + scaled_sq) * sigma)
    first, second, third = split3(grad)
    grads[0] = first.astype(f32)
    grads[1] = second.astype(f32)
    grads[2] = third.astype(f32)

    sums = []
    for t in range(2):
        def scatter_step(c, total):
            at = pl.ds(pl.multiple_of(c * CHUNK, CHUNK), CHUNK)
            hot = row_id == where_row[t:t + 1, at]
            left = jnp.concatenate(
                [jnp.where(hot, grads[k, t:t + 1, at], 0.0).astype(jnp.bfloat16) for k in range(3)],
                axis=0)
            right = jnp.where(lane_id == where_lane[t:t + 1, at], 1.0, 0.0).astype(jnp.bfloat16)
            return total + lax.dot_general(left, right, (((1,), (1,)), ((), ())),
                                           preferred_element_type=f32)
        total = lax.fori_loop(0, OBS // CHUNK, scatter_step, jnp.zeros((3 * ROWS, 128), f32))
        sums.append(total[0:ROWS] + total[ROWS:2 * ROWS] + total[2 * ROWS:3 * ROWS])
    update = jnp.concatenate(sums, axis=0).astype(jnp.bfloat16).astype(f32)
    columns = jnp.transpose(update)

    def backward(cols, start, width):
        for half in range(width // 64):
            total = jnp.zeros((64, 256), f32)
            for k in range(8):
                j = k // LEV * ROWS + k % LEV * BLOCKS
                weight = cols[half * 64:(half + 1) * 64, j:j + 1]
                total = total + p_ref[k, pl.ds(start + half * 64, 64), :].astype(f32) * weight
            yield total

    def backward_step(blk, carry):
        start = pl.multiple_of(blk * 128, 128)
        cols = pltpu.roll(columns, 128 - blk, axis=1)
        total = jnp.concatenate(list(backward(cols, start, 128)), axis=0)
        adj_ref[:, pl.ds(start, 128)] = jnp.transpose(total).astype(jnp.bfloat16)
        return carry

    lax.fori_loop(0, 12, backward_step, 0)
    cols = pltpu.roll(columns, 128 - 12, axis=1)
    (total,) = backward(cols, 1536, 64)
    adj_ref[:, 1536:1600] = jnp.transpose(total).astype(jnp.bfloat16)


def middle(cases, fields, obs_index, innovation, obs_sigma, qc_class):
    vm = pl.BlockSpec(memory_space=pltpu.VMEM)
    return pl.pallas_call(
        middle_kernel,
        out_shape=(jax.ShapeDtypeStruct((256, PIECE), jnp.bfloat16),
                   jax.ShapeDtypeStruct((1, 1), jnp.float32)),
        in_specs=[vm] * 6,
        out_specs=(vm, vm),
        scratch_shapes=[
            pltpu.VMEM((2, ROWS, 128), jnp.float32),
            pltpu.VMEM((2, 128, 3 * ROWS), jnp.bfloat16),
            pltpu.VMEM((2, OBS), jnp.float32),
            pltpu.VMEM((3, 2, OBS), jnp.float32),
            pltpu.VMEM((2, OBS), jnp.int32),
            pltpu.VMEM((2, OBS), jnp.int32),
        ],
        compiler_params=pltpu.CompilerParams(vmem_limit_bytes=40 * 1024 * 1024),
        name="middle",
    )(cases, fields, obs_index, innovation, obs_sigma, qc_class)


def joined_along(tiles, dim):
    lengths = list(tiles.shape[1:])
    lengths[dim] *= tiles.shape[0]
    return jnp.moveaxis(tiles, 0, dim).reshape(lengths)


def from_everyone(value, axis):
    copies = jnp.broadcast_to(value, (lax.axis_size(axis), *value.shape))
    return lax.all_to_all(copies, axis, split_axis=0, concat_axis=0, tiled=True)


def gather_directly(value, axis, dim):
    return joined_along(from_everyone(value, axis), dim)


def cut_along(value, dim, count):
    lengths = value.shape
    tiles = value.reshape(*lengths[:dim], count, lengths[dim] // count, *lengths[dim + 1 :])
    return jnp.moveaxis(tiles, dim, 0)


def sent_and_summed(value, axis, dim):
    tiles = cut_along(value, dim, lax.axis_size(axis))
    arrived = lax.all_to_all(tiles, axis, split_axis=0, concat_axis=0, tiled=True)
    return arrived.astype(jnp.float32).sum(axis=0)


def lookup_tables(segment_length):
    wave_num = jnp.arange(segment_length, dtype=jnp.float32)[:, None]
    grid_positions = jnp.arange(segment_length, dtype=jnp.float32)[None, :]
    basis = jnp.cos(jnp.pi * (grid_positions + 0.5) * wave_num / segment_length) * jnp.sqrt(
        2.0 / segment_length
    )
    return jnp.where(wave_num == 0, basis * jnp.sqrt(0.5), basis)


def synthesize(control, spectrum, basis_x, basis_y):
    coeffs = (control * spectrum[None, :]).reshape(control.shape[0], GX, GY)
    middle = jnp.einsum("kn,mkl->mnl", basis_x, coeffs, precision=lax.Precision.HIGHEST)
    result = jnp.einsum("mnl,lp->mnp", middle, basis_y, precision=lax.Precision.HIGHEST)
    return result.reshape(control.shape[0], GX * GY)


def analyze(adjoint, spectrum, basis_x, basis_y):
    state_fields = adjoint.reshape(adjoint.shape[0], GX, GY)
    middle = jnp.einsum("kn,mnp->mkp", basis_x, state_fields, precision=lax.Precision.HIGHEST)
    result = jnp.einsum("mkp,lp->mkl", middle, basis_y, precision=lax.Precision.HIGHEST)
    return result.reshape(adjoint.shape[0], GX * GY) * spectrum[None, :]


def per_device(control, spectrum, perturb, obs_index, innovation, obs_sigma, qc_class):
    basis_x = lookup_tables(GX)
    basis_y = lookup_tables(GY)
    cases = perturb.transpose(0, 2, 3, 1).reshape(2 * LEV, PIECE, 256)
    member_field = synthesize(control, spectrum, basis_x, basis_y).astype(jnp.bfloat16)
    pieces = lax.all_to_all(member_field, SPACE, split_axis=1, concat_axis=0, tiled=True)
    fields = gather_directly(pieces, TM, 0)
    partial, obs_part = middle(cases, fields, obs_index, innovation, obs_sigma, qc_class)
    back_part = 0.5 * jnp.sum(control * control)
    summed_rows = sent_and_summed(partial, TM, 0)
    adjoint = lax.all_to_all(
        summed_rows.astype(jnp.bfloat16), SPACE, split_axis=0, concat_axis=1, tiled=True
    ).astype(summed_rows.dtype)
    gradient = control + analyze(adjoint, spectrum, basis_x, basis_y)
    grad_part = jnp.sum(gradient * gradient)
    mine = jnp.stack([obs_part[0, 0] + back_part, grad_part]).reshape(1, 1, 2)
    mine = jnp.broadcast_to(mine, (256, 1, 2))
    sums = lax.all_to_all(mine, TM_SPACE, split_axis=0, concat_axis=0, tiled=True).sum(axis=(0, 1))
    total_cost = sums[0]
    step_size = 0.5 * total_cost / (sums[1] + 1e-06)
    return (control - step_size * gradient, total_cost.reshape(1))


def solution(mesh):
    split = Mesh(
        mesh.devices.reshape(2, 4, 4, 4, 2), ("tm_0", "tm_1", "space_0", "space_1", "space_2")
    )
    return jax.shard_map(
        per_device,
        mesh=split,
        in_specs=(
            P(TM_SPACE, None),
            P(),
            P(TM, None, None, SPACE),
            P(TM, SPACE),
            P(TM, SPACE),
            P(TM, SPACE),
            P(TM, SPACE),
        ),
        out_specs=(P(TM_SPACE, None), P()),
        check_vma=False,
    )
```

```python
import jax
import jax.numpy as jnp
import ml_dtypes
import numpy as np
from jax import lax
from jax.experimental import pallas as pl
from jax.experimental.pallas import tpu as pltpu
from jax.sharding import Mesh
from jax.sharding import PartitionSpec as P

PIECE = 1600
LEV = 4
BLOCKS = 13
ROWS = 64
OBS = 2048
CHUNK = 256


def split3(value):
    first = value.astype(jnp.bfloat16)
    rest = value - first.astype(jnp.float32)
    second = rest.astype(jnp.bfloat16)
    third = (rest - second.astype(jnp.float32)).astype(jnp.bfloat16)
    return first, second, third


def middle_kernel(p_ref, f_ref, idx_ref, inn_ref, sig_ref, qc_ref, adj_ref, cost_ref,
                  cells, table, modelled, grads, where_row, where_lane):
    f32 = jnp.float32
    cells[...] = jnp.zeros_like(cells)

    def forward(blk, start, width):
        rows = p_ref[:, start:start + width, :].reshape(8 * width, 256)
        prod = jnp.dot(rows, f_ref[:, start:start + width], preferred_element_type=f32)
        same = lax.broadcasted_iota(jnp.int32, (width, width), 0) == lax.broadcasted_iota(
            jnp.int32, (width, width), 1)
        for k in range(8):
            one = jnp.where(same, prod[k * width:(k + 1) * width], 0.0)
            row = jnp.sum(one, axis=0, keepdims=True)
            at = k % LEV * BLOCKS + blk
            cells[k // LEV, at:at + 1, 0:width] = row

    for blk in range(BLOCKS):
        forward(blk, blk * 128, min(128, PIECE - blk * 128))

    index = idx_ref[...]
    level = ((index >= PIECE).astype(jnp.int32) + (index >= 2 * PIECE).astype(jnp.int32)
             + (index >= 3 * PIECE).astype(jnp.int32))
    point = index - level * PIECE
    where_row[...] = level * BLOCKS + (point >> 7)
    where_lane[...] = point & 127

    for t in range(2):
        parts = split3(jnp.transpose(cells[t]))
        for k in range(3):
            table[t, :, k * ROWS:(k + 1) * ROWS] = parts[k]

    row_id = lax.broadcasted_iota(jnp.int32, (ROWS, CHUNK), 0)
    lane_id = lax.broadcasted_iota(jnp.int32, (128, CHUNK), 0)

    for t in range(2):
        for c in range(OBS // CHUNK):
            at = slice(c * CHUNK, (c + 1) * CHUNK)
            hot = jnp.where(row_id == where_row[t:t + 1, at], 1.0, 0.0).astype(jnp.bfloat16)
            hot = jnp.concatenate([hot, hot, hot], axis=0)
            lines = jnp.dot(table[t], hot, preferred_element_type=f32)
            lines = jnp.where(lane_id == where_lane[t:t + 1, at], lines, 0.0)
            modelled[t:t + 1, at] = jnp.sum(lines, axis=0, keepdims=True)

    sigma = sig_ref[...]
    kind = qc_ref[...]
    radius_sq = jnp.where(kind == 0, 16.0, jnp.where(kind == 1, 4.0, 1.0))
    scaled = (modelled[...] - inn_ref[...]) / sigma
    scaled_sq = scaled * scaled / radius_sq
    terms = 0.5 * radius_sq * jnp.log1p(scaled_sq)
    cost_ref[...] = jnp.sum(terms, axis=(0, 1), keepdims=True)
    grad = scaled / ((1.0 + scaled_sq) * sigma)
    first, second, third = split3(grad)
    grads[0] = first.astype(f32)
    grads[1] = second.astype(f32)
    grads[2] = third.astype(f32)

    sums = []
    for t in range(2):
        total = jnp.zeros((3 * ROWS, 128), f32)
        for c in range(OBS // CHUNK):
            at = slice(c * CHUNK, (c + 1) * CHUNK)
            hot = row_id == where_row[t:t + 1, at]
            left = jnp.concatenate(
                [jnp.where(hot, grads[k, t:t + 1, at], 0.0).astype(jnp.bfloat16) for k in range(3)],
                axis=0)
            right = jnp.where(lane_id == where_lane[t:t + 1, at], 1.0, 0.0).astype(jnp.bfloat16)
            total = total + lax.dot_general(left, right, (((1,), (1,)), ((), ())),
                                            preferred_element_type=f32)
        sums.append(total[0:ROWS] + total[ROWS:2 * ROWS] + total[2 * ROWS:3 * ROWS])
    update = jnp.concatenate(sums, axis=0).astype(jnp.bfloat16).astype(f32)
    columns = jnp.transpose(update)

    for blk in range(BLOCKS):
        start = blk * 128
        width = min(128, PIECE - start)
        halves = []
        for half in range(width // 64):
            lanes = slice(half * 64, half * 64 + 64)
            points = slice(start + half * 64, start + half * 64 + 64)
            total = jnp.zeros((64, 256), f32)
            for k in range(8):
                j = k // LEV * ROWS + k % LEV * BLOCKS + blk
                total = total + p_ref[k, points, :].astype(f32) * columns[lanes, j:j + 1]
            halves.append(total)
        total = jnp.concatenate(halves, axis=0)
        adj_ref[:, start:start + width] = jnp.transpose(total).astype(jnp.bfloat16)


def middle(cases, fields, obs_index, innovation, obs_sigma, qc_class):
    vm = pl.BlockSpec(memory_space=pltpu.VMEM)
    return pl.pallas_call(
        middle_kernel,
        out_shape=(jax.ShapeDtypeStruct((256, PIECE), jnp.bfloat16),
                   jax.ShapeDtypeStruct((1, 1), jnp.float32)),
        in_specs=[vm] * 6,
        out_specs=(vm, vm),
        scratch_shapes=[
            pltpu.VMEM((2, ROWS, 128), jnp.float32),
            pltpu.VMEM((2, 128, 3 * ROWS), jnp.bfloat16),
            pltpu.VMEM((2, OBS), jnp.float32),
            pltpu.VMEM((3, 2, OBS), jnp.float32),
            pltpu.VMEM((2, OBS), jnp.int32),
            pltpu.VMEM((2, OBS), jnp.int32),
        ],
        compiler_params=pltpu.CompilerParams(vmem_limit_bytes=40 * 1024 * 1024),
        name="middle",
    )(cases, fields, obs_index, innovation, obs_sigma, qc_class)


F32 = jnp.float32
BF16 = jnp.bfloat16
GX = 320
GY = 160
MEMBERS = 256
WIDE = 16 * 128
SPACE = ("space_0", "space_1", "space_2")
TM = ("tm_0", "tm_1")
TM_SPACE = ("tm_0", "tm_1", "space_0", "space_1", "space_2")


def two_parts(value):
    high = np.asarray(value, np.float32).astype(ml_dtypes.bfloat16)
    low = (value - high.astype(np.float64)).astype(np.float32).astype(ml_dtypes.bfloat16)
    return high, low


def lookup_table(length):
    wave = np.arange(length)[:, None]
    angle = np.pi * (np.arange(length)[None, :] + 0.5) * wave / length
    return np.cos(angle) * np.sqrt(np.where(wave == 0, 1.0, 2.0) / length)


def split2(value):
    high = value.astype(BF16)
    return high, (value - high.astype(F32)).astype(BF16)


def product(left, right):
    (left_high, left_low), (right_high, right_low) = left, right
    return (jnp.dot(left_high, right_high, preferred_element_type=F32)
            + (jnp.dot(left_low, right_high, preferred_element_type=F32)
               + jnp.dot(left_high, right_low, preferred_element_type=F32)))


def first_kernel(c_ref, s_ref, x_hbm, y_hbm, cases_hbm, out_ref, back_ref, cases_ref, wide, tall, x_ref, y_ref, sems):
    copies = [
        pltpu.make_async_copy(y_hbm, y_ref, sems.at[0]),
        pltpu.make_async_copy(x_hbm, x_ref, sems.at[1]),
        pltpu.make_async_copy(cases_hbm, cases_ref, sems.at[2]),
    ]
    for copy in copies:
        copy.start()
    control = c_ref[...]
    back_ref[...] = 0.5 * jnp.sum(control * control, axis=(0, 1), keepdims=True)
    coeffs = split2(control * s_ref[...])
    wide[:, PIECE:] = jnp.zeros((32, wide.shape[1] - PIECE), F32)
    copies[0].wait()
    rows = split2(product(coeffs, (y_ref[0], y_ref[1])))
    copies[1].wait()
    field = product((x_ref[0], x_ref[1]), rows)
    for i in range(10):
        wide[:, i * GY:(i + 1) * GY] = field[i * 32:(i + 1) * 32]
    for r in range(BLOCKS):
        tall[:, r, :] = wide[:, r * 128:(r + 1) * 128]
    for r in range(BLOCKS, 16):
        tall[:, r, :] = jnp.zeros((32, 128), F32)
    out_ref[...] = tall[...].astype(BF16)
    copies[2].wait()


def spread_kernel(in_ref, out_ref, tall, wide):
    tall[...] = in_ref[...].astype(F32)
    for r in range(BLOCKS):
        wide[:, r * 128:(r + 1) * 128] = tall[:, r, :]
    value = wide[:, 0:PIECE].astype(BF16)
    for k in range(8):
        out_ref[k] = value


def fold_kernel(in_ref, out_ref, tall, wide):
    total = in_ref[0].astype(F32)
    for k in range(1, 8):
        total = total + in_ref[k].astype(F32)
    wide[:, 0:PIECE] = total
    wide[:, PIECE:] = jnp.zeros((32, wide.shape[1] - PIECE), F32)
    for r in range(BLOCKS):
        tall[:, r, :] = wide[:, r * 128:(r + 1) * 128]
    for r in range(BLOCKS, 16):
        tall[:, r, :] = jnp.zeros((32, 128), F32)
    out_ref[...] = tall[...].astype(BF16)


def last_kernel(in_ref, c_ref, s_ref, xh, xl, yh, yl, back_ref, obs_ref, grad_ref, pay_ref, tall, wide, adj):
    tall[...] = in_ref[...].astype(F32)
    for r in range(BLOCKS):
        wide[:, r * 128:(r + 1) * 128] = tall[:, r, :]
    for i in range(10):
        adj[i * 32:(i + 1) * 32, :] = wide[:, i * GY:(i + 1) * GY].astype(BF16)
    part = adj[...]
    rows = (jnp.dot(xh[...], part, preferred_element_type=F32)
            + jnp.dot(xl[...], part, preferred_element_type=F32))
    grad = c_ref[...] + s_ref[...] * product(split2(rows), (yh[...], yl[...]))
    grad_ref[...] = grad
    cost = back_ref[...] + obs_ref[...]
    norm = jnp.sum(grad * grad, axis=(0, 1), keepdims=True)
    lane = lax.broadcasted_iota(jnp.int32, (MEMBERS, 128), 1)
    pay_ref[...] = jnp.where(lane == 0, cost, jnp.where(lane == 1, norm, 0.0))


def step_kernel(pay_ref, c_ref, g_ref, out_ref, cost_ref):
    sums = jnp.sum(pay_ref[...], axis=0, keepdims=True)
    cost = sums[:, 0:1]
    size = 0.5 * cost / (sums[:, 1:2] + 1e-06)
    out_ref[...] = c_ref[...] - size * g_ref[...]
    cost_ref[...] = cost


def call(kernel, outs, scratch, name, specs=None):
    vm = pl.BlockSpec(memory_space=pltpu.VMEM)

    def run(*args):
        ins = [vm] * len(args)
        for at in specs or ():
            ins[at] = pl.BlockSpec(memory_space=pltpu.HBM)
        return pl.pallas_call(
            kernel,
            out_shape=tuple(jax.ShapeDtypeStruct(*out) for out in outs),
            in_specs=ins,
            out_specs=(vm,) * len(outs),
            scratch_shapes=scratch,
            compiler_params=pltpu.CompilerParams(vmem_limit_bytes=40 * 1024 * 1024),
            name=name,
        )(*args)

    return run


def exchanged(value, axis):
    return lax.all_to_all(value, axis, split_axis=0, concat_axis=0, tiled=True)


def per_device(control, spectrum, perturb, obs_index, innovation, obs_sigma, qc_class):
    order = np.arange(GX).reshape(32, 10).T.reshape(-1)
    table_x = lookup_table(GX)[:, order]
    table_y = lookup_table(GY)
    cases = perturb.transpose(0, 2, 3, 1).reshape(2 * LEV, PIECE, MEMBERS)
    control_grid = control.reshape(GX, GY)
    spectrum_grid = spectrum.reshape(GX, GY)
    tall = pltpu.VMEM((32, 16, 128), F32)
    wide = pltpu.VMEM((32, BLOCKS * 128), F32)

    sent, back, cases = call(
        first_kernel,
        (((32, 16, 128), BF16), ((1, 1), F32), (cases.shape, BF16)),
        [wide, tall, pltpu.VMEM((2, GX, GX), BF16), pltpu.VMEM((2, GY, GY), BF16),
         pltpu.SemaphoreType.DMA((3,))],
        "synthesis", specs=(2, 3, 4),
    )(control_grid, spectrum_grid, np.stack(two_parts(table_x.T)), np.stack(two_parts(table_y)), cases)
    pieces = exchanged(sent, SPACE)
    (copies,) = call(spread_kernel, (((8, 32, PIECE), BF16),), [tall, wide], "spread")(pieces)
    fields = exchanged(copies, TM).reshape(MEMBERS, PIECE)
    partial, obs = middle(cases, fields, obs_index, innovation, obs_sigma, qc_class)
    terms = exchanged(partial.reshape(8, 32, PIECE), TM)
    (summed,) = call(fold_kernel, (((32, 16, 128), BF16),), [tall, wide], "fold")(terms)
    adjoint = exchanged(summed, SPACE)
    gradient, mine = call(
        last_kernel,
        (((GX, GY), F32), ((MEMBERS, 128), F32)),
        [tall, wide, pltpu.VMEM((GX, GY), BF16)],
        "analysis",
    )(adjoint, control_grid, spectrum_grid, *two_parts(table_x), *two_parts(table_y.T), back, obs)
    sums = exchanged(mine.reshape(MEMBERS, 1, 128), TM_SPACE).reshape(MEMBERS, 128)
    result, cost = call(
        step_kernel, (((400, 128), F32), ((1, 1), F32)), [], "step"
    )(sums, control.reshape(400, 128), gradient.reshape(400, 128))
    return result.reshape(1, GX * GY), cost.reshape(1)


def solution(mesh):
    split = Mesh(
        mesh.devices.reshape(2, 4, 4, 4, 2), ("tm_0", "tm_1", "space_0", "space_1", "space_2")
    )
    return jax.shard_map(
        per_device,
        mesh=split,
        in_specs=(
            P(TM_SPACE, None),
            P(),
            P(TM, None, None, SPACE),
            P(TM, SPACE),
            P(TM, SPACE),
            P(TM, SPACE),
            P(TM, SPACE),
        ),
        out_specs=(P(TM_SPACE, None), P()),
        check_vma=False,
    )
```

```python
import jax
import jax.numpy as jnp
import ml_dtypes
import numpy as np
from jax import lax
from jax.experimental import pallas as pl
from jax.experimental.pallas import tpu as pltpu
from jax.sharding import Mesh
from jax.sharding import PartitionSpec as P

PIECE = 1600
LEV = 4
BLOCKS = 13
ROWS = 64
OBS = 2048
CHUNK = 256


def split3(value):
    first = value.astype(jnp.bfloat16)
    rest = value - first.astype(jnp.float32)
    second = rest.astype(jnp.bfloat16)
    third = (rest - second.astype(jnp.float32)).astype(jnp.bfloat16)
    return first, second, third


def middle_kernel(p_ref, f_ref, idx_ref, inn_ref, sig_ref, qc_ref, adj_ref, cost_ref,
                  cells, table, modelled, grads, where_row, where_lane):
    f32 = jnp.float32
    cells[...] = jnp.zeros_like(cells)

    def forward(blk, start, width):
        rows = p_ref[:, start:start + width, :].reshape(8 * width, 256)
        prod = jnp.dot(rows, f_ref[:, start:start + width], preferred_element_type=f32)
        same = lax.broadcasted_iota(jnp.int32, (width, width), 0) == lax.broadcasted_iota(
            jnp.int32, (width, width), 1)
        for k in range(8):
            one = jnp.where(same, prod[k * width:(k + 1) * width], 0.0)
            row = jnp.sum(one, axis=0, keepdims=True)
            at = k % LEV * BLOCKS + blk
            cells[k // LEV, at:at + 1, 0:width] = row

    for blk in range(BLOCKS):
        forward(blk, blk * 128, min(128, PIECE - blk * 128))

    index = idx_ref[...]
    level = ((index >= PIECE).astype(jnp.int32) + (index >= 2 * PIECE).astype(jnp.int32)
             + (index >= 3 * PIECE).astype(jnp.int32))
    point = index - level * PIECE
    where_row[...] = level * BLOCKS + (point >> 7)
    where_lane[...] = point & 127

    for t in range(2):
        parts = split3(jnp.transpose(cells[t]))
        for k in range(3):
            table[t, :, k * ROWS:(k + 1) * ROWS] = parts[k]

    row_id = lax.broadcasted_iota(jnp.int32, (ROWS, CHUNK), 0)
    lane_id = lax.broadcasted_iota(jnp.int32, (128, CHUNK), 0)

    for t in range(2):
        for c in range(OBS // CHUNK):
            at = slice(c * CHUNK, (c + 1) * CHUNK)
            hot = jnp.where(row_id == where_row[t:t + 1, at], 1.0, 0.0).astype(jnp.bfloat16)
            hot = jnp.concatenate([hot, hot, hot], axis=0)
            lines = jnp.dot(table[t], hot, preferred_element_type=f32)
            lines = jnp.where(lane_id == where_lane[t:t + 1, at], lines, 0.0)
            modelled[t:t + 1, at] = jnp.sum(lines, axis=0, keepdims=True)

    sigma = sig_ref[...]
    kind = qc_ref[...]
    radius_sq = jnp.where(kind == 0, 16.0, jnp.where(kind == 1, 4.0, 1.0))
    scaled = (modelled[...] - inn_ref[...]) / sigma
    scaled_sq = scaled * scaled / radius_sq
    terms = 0.5 * radius_sq * jnp.log1p(scaled_sq)
    cost_ref[...] = jnp.sum(terms, axis=(0, 1), keepdims=True)
    grad = scaled / ((1.0 + scaled_sq) * sigma)
    first, second, third = split3(grad)
    grads[0] = first.astype(f32)
    grads[1] = second.astype(f32)
    grads[2] = third.astype(f32)

    sums = []
    for t in range(2):
        total = jnp.zeros((3 * ROWS, 128), f32)
        for c in range(OBS // CHUNK):
            at = slice(c * CHUNK, (c + 1) * CHUNK)
            hot = row_id == where_row[t:t + 1, at]
            left = jnp.concatenate(
                [jnp.where(hot, grads[k, t:t + 1, at], 0.0).astype(jnp.bfloat16) for k in range(3)],
                axis=0)
            right = jnp.where(lane_id == where_lane[t:t + 1, at], 1.0, 0.0).astype(jnp.bfloat16)
            total = total + lax.dot_general(left, right, (((1,), (1,)), ((), ())),
                                            preferred_element_type=f32)
        sums.append(total[0:ROWS] + total[ROWS:2 * ROWS] + total[2 * ROWS:3 * ROWS])
    update = jnp.concatenate(sums, axis=0).astype(jnp.bfloat16).astype(f32)
    columns = jnp.transpose(update)

    for blk in range(BLOCKS):
        start = blk * 128
        width = min(128, PIECE - start)
        halves = []
        for half in range(width // 64):
            lanes = slice(half * 64, half * 64 + 64)
            points = slice(start + half * 64, start + half * 64 + 64)
            total = jnp.zeros((64, 256), f32)
            for k in range(8):
                j = k // LEV * ROWS + k % LEV * BLOCKS + blk
                total = total + p_ref[k, points, :].astype(f32) * columns[lanes, j:j + 1]
            halves.append(total)
        total = jnp.concatenate(halves, axis=0)
        adj_ref[:, start:start + width] = jnp.transpose(total).astype(jnp.bfloat16)


def middle(cases, fields, obs_index, innovation, obs_sigma, qc_class):
    vm = pl.BlockSpec(memory_space=pltpu.VMEM)
    return pl.pallas_call(
        middle_kernel,
        out_shape=(jax.ShapeDtypeStruct((256, PIECE), jnp.bfloat16),
                   jax.ShapeDtypeStruct((1, 1), jnp.float32)),
        in_specs=[vm] * 6,
        out_specs=(vm, vm),
        scratch_shapes=[
            pltpu.VMEM((2, ROWS, 128), jnp.float32),
            pltpu.VMEM((2, 128, 3 * ROWS), jnp.bfloat16),
            pltpu.VMEM((2, OBS), jnp.float32),
            pltpu.VMEM((3, 2, OBS), jnp.float32),
            pltpu.VMEM((2, OBS), jnp.int32),
            pltpu.VMEM((2, OBS), jnp.int32),
        ],
        compiler_params=pltpu.CompilerParams(vmem_limit_bytes=40 * 1024 * 1024),
        name="middle",
    )(cases, fields, obs_index, innovation, obs_sigma, qc_class)


F32 = jnp.float32
BF16 = jnp.bfloat16
GX = 320
GY = 160
MEMBERS = 256
WIDE = 16 * 128
SPACE = ("space_0", "space_1", "space_2")
TM = ("tm_0", "tm_1")
TM_SPACE = ("tm_0", "tm_1", "space_0", "space_1", "space_2")


def two_parts(value):
    high = np.asarray(value, np.float32).astype(ml_dtypes.bfloat16)
    low = (value - high.astype(np.float64)).astype(np.float32).astype(ml_dtypes.bfloat16)
    return high, low


def lookup_table(length):
    wave = np.arange(length)[:, None]
    angle = np.pi * (np.arange(length)[None, :] + 0.5) * wave / length
    return np.cos(angle) * np.sqrt(np.where(wave == 0, 1.0, 2.0) / length)


def split2(value):
    high = value.astype(BF16)
    return high, (value - high.astype(F32)).astype(BF16)


def product(left, right):
    (left_high, left_low), (right_high, right_low) = left, right
    return (jnp.dot(left_high, right_high, preferred_element_type=F32)
            + (jnp.dot(left_low, right_high, preferred_element_type=F32)
               + jnp.dot(left_high, right_low, preferred_element_type=F32)))


def rows_of(flat, lines, grid):
    for k in range(5):
        lines[:, k * 128:(k + 1) * 128] = flat[pl.ds(k, 80, stride=5), :]
    for k in range(4):
        grid[k * 80:(k + 1) * 80, :] = lines[:, k * GY:(k + 1) * GY]


def flat_of(grid, lines, flat):
    for k in range(4):
        lines[:, k * GY:(k + 1) * GY] = grid[k * 80:(k + 1) * 80, :]
    for k in range(5):
        flat[pl.ds(k, 80, stride=5), :] = lines[:, k * 128:(k + 1) * 128]


def first_kernel(c_hbm, s_hbm, x_hbm, y_hbm, cases_hbm, out_ref, back_ref, cases_ref,
                 wide, tall, lines, grid, c_ref, s_ref, x_ref, y_ref, sems):
    pairs = ((c_hbm, c_ref), (s_hbm, s_ref), (y_hbm, y_ref), (x_hbm, x_ref), (cases_hbm, cases_ref))
    copies = [pltpu.make_async_copy(*pair, sems.at[k]) for k, pair in enumerate(pairs)]
    for copy in copies:
        copy.start()
    wide[:, PIECE:] = jnp.zeros((32, wide.shape[1] - PIECE), F32)
    copies[0].wait()
    control = c_ref[...]
    back_ref[...] = 0.5 * jnp.sum(control * control, axis=(0, 1), keepdims=True)
    copies[1].wait()
    c_ref[...] = control * s_ref[...]
    rows_of(c_ref, lines, grid)
    coeffs = split2(grid[...])
    copies[2].wait()
    rows = split2(product(coeffs, (y_ref[0], y_ref[1])))
    copies[3].wait()
    field = product((x_ref[0], x_ref[1]), rows)
    for i in range(10):
        wide[:, i * GY:(i + 1) * GY] = field[i * 32:(i + 1) * 32]
    for r in range(BLOCKS):
        tall[:, r, :] = wide[:, r * 128:(r + 1) * 128]
    for r in range(BLOCKS, 16):
        tall[:, r, :] = jnp.zeros((32, 128), F32)
    out_ref[...] = tall[...].astype(BF16)
    copies[4].wait()


def spread_kernel(in_ref, out_ref, tall, wide):
    tall[...] = in_ref[...].astype(F32)
    for r in range(BLOCKS):
        wide[:, r * 128:(r + 1) * 128] = tall[:, r, :]
    value = wide[:, 0:PIECE].astype(BF16)
    for k in range(8):
        out_ref[k] = value


def fold_kernel(in_ref, out_ref, tall, wide):
    total = in_ref[0].astype(F32)
    for k in range(1, 8):
        total = total + in_ref[k].astype(F32)
    wide[:, 0:PIECE] = total
    wide[:, PIECE:] = jnp.zeros((32, wide.shape[1] - PIECE), F32)
    for r in range(BLOCKS):
        tall[:, r, :] = wide[:, r * 128:(r + 1) * 128]
    for r in range(BLOCKS, 16):
        tall[:, r, :] = jnp.zeros((32, 128), F32)
    out_ref[...] = tall[...].astype(BF16)


def last_kernel(in_ref, c_ref, s_ref, xh, xl, yh, yl, back_ref, obs_ref, grad_ref, pay_ref,
                tall, wide, adj, lines, grid):
    tall[...] = in_ref[...].astype(F32)
    for r in range(BLOCKS):
        wide[:, r * 128:(r + 1) * 128] = tall[:, r, :]
    for i in range(10):
        adj[i * 32:(i + 1) * 32, :] = wide[:, i * GY:(i + 1) * GY].astype(BF16)
    part = adj[...]
    rows = (jnp.dot(xh[...], part, preferred_element_type=F32)
            + jnp.dot(xl[...], part, preferred_element_type=F32))
    grid[...] = product(split2(rows), (yh[...], yl[...]))
    flat_of(grid, lines, grad_ref)
    grad = c_ref[...] + s_ref[...] * grad_ref[...]
    grad_ref[...] = grad
    cost = back_ref[...] + obs_ref[...]
    norm = jnp.sum(grad * grad, axis=(0, 1), keepdims=True)
    lane = lax.broadcasted_iota(jnp.int32, (MEMBERS, 128), 1)
    pay_ref[...] = jnp.where(lane == 0, cost, jnp.where(lane == 1, norm, 0.0))


def step_kernel(pay_ref, c_ref, g_ref, out_ref, cost_ref):
    sums = jnp.sum(pay_ref[...], axis=0, keepdims=True)
    cost = sums[:, 0:1]
    size = 0.5 * cost / (sums[:, 1:2] + 1e-06)
    out_ref[...] = c_ref[...] - size * g_ref[...]
    cost_ref[...] = cost


def call(kernel, outs, scratch, name, specs=None):
    vm = pl.BlockSpec(memory_space=pltpu.VMEM)

    def run(*args):
        ins = [vm] * len(args)
        for at in specs or ():
            ins[at] = pl.BlockSpec(memory_space=pltpu.HBM)
        return pl.pallas_call(
            kernel,
            out_shape=tuple(jax.ShapeDtypeStruct(*out) for out in outs),
            in_specs=ins,
            out_specs=(vm,) * len(outs),
            scratch_shapes=scratch,
            compiler_params=pltpu.CompilerParams(vmem_limit_bytes=40 * 1024 * 1024),
            name=name,
        )(*args)

    return run


def exchanged(value, axis):
    return lax.all_to_all(value, axis, split_axis=0, concat_axis=0, tiled=True)


def per_device(control, spectrum, perturb, obs_index, innovation, obs_sigma, qc_class):
    waves = np.arange(GX).reshape(80, 4).T.reshape(-1)
    points = np.arange(GX).reshape(32, 10).T.reshape(-1)
    table_x = lookup_table(GX)[waves][:, points]
    table_y = lookup_table(GY)
    cases = perturb.transpose(0, 2, 3, 1).reshape(2 * LEV, PIECE, MEMBERS)
    control_flat = control.reshape(400, 128)
    spectrum_flat = spectrum.reshape(400, 128)
    tall = pltpu.VMEM((32, 16, 128), F32)
    wide = pltpu.VMEM((32, BLOCKS * 128), F32)
    lines = pltpu.VMEM((80, 640), F32)
    grid = pltpu.VMEM((GX, GY), F32)
    flat = pltpu.VMEM((400, 128), F32)

    inputs = (control_flat, spectrum_flat, jnp.asarray(np.stack(two_parts(table_x.T))),
              jnp.asarray(np.stack(two_parts(table_y))), cases)
    sent, back, cases = call(
        first_kernel,
        (((32, 16, 128), BF16), ((1, 1), F32), (cases.shape, BF16)),
        [wide, tall, lines, grid, flat, flat, pltpu.VMEM((2, GX, GX), BF16),
         pltpu.VMEM((2, GY, GY), BF16), pltpu.SemaphoreType.DMA((5,))],
        "synthesis", specs=range(5),
    )(*[pltpu.with_memory_space_constraint(value, pltpu.HBM) for value in inputs])
    pieces = exchanged(sent, SPACE)
    (copies,) = call(spread_kernel, (((8, 32, PIECE), BF16),), [tall, wide], "spread")(pieces)
    fields = exchanged(copies, TM).reshape(MEMBERS, PIECE)
    partial, obs = middle(cases, fields, obs_index, innovation, obs_sigma, qc_class)
    terms = exchanged(partial.reshape(8, 32, PIECE), TM)
    (summed,) = call(fold_kernel, (((32, 16, 128), BF16),), [tall, wide], "fold")(terms)
    adjoint = exchanged(summed, SPACE)
    gradient, mine = call(
        last_kernel,
        (((400, 128), F32), ((MEMBERS, 128), F32)),
        [tall, wide, pltpu.VMEM((GX, GY), BF16), lines, grid],
        "analysis",
    )(adjoint, control_flat, spectrum_flat, *two_parts(table_x), *two_parts(table_y.T), back, obs)
    sums = exchanged(mine.reshape(MEMBERS, 1, 128), TM_SPACE).reshape(MEMBERS, 128)
    result, cost = call(
        step_kernel, (((400, 128), F32), ((1, 1), F32)), [], "step"
    )(sums, control_flat, gradient)
    return result.reshape(1, GX * GY), cost.reshape(1)


def solution(mesh):
    split = Mesh(
        mesh.devices.reshape(2, 4, 4, 4, 2), ("tm_0", "tm_1", "space_0", "space_1", "space_2")
    )
    return jax.shard_map(
        per_device,
        mesh=split,
        in_specs=(
            P(TM_SPACE, None),
            P(),
            P(TM, None, None, SPACE),
            P(TM, SPACE),
            P(TM, SPACE),
            P(TM, SPACE),
            P(TM, SPACE),
        ),
        out_specs=(P(TM_SPACE, None), P()),
        check_vma=False,
    )
```

```python
import jax
import jax.numpy as jnp
import ml_dtypes
import numpy as np
from jax import lax
from jax.experimental import pallas as pl
from jax.experimental.pallas import tpu as pltpu
from jax.sharding import Mesh
from jax.sharding import PartitionSpec as P

PIECE = 1600
LEV = 4
BLOCKS = 13
ROWS = 64
OBS = 2048
CHUNK = 256
EARLY = 1024


def split3(value):
    first = value.astype(jnp.bfloat16)
    rest = value - first.astype(jnp.float32)
    second = rest.astype(jnp.bfloat16)
    third = (rest - second.astype(jnp.float32)).astype(jnp.bfloat16)
    return first, second, third


def middle_kernel(early_ref, cases_hbm, f_ref, idx_ref, inn_ref, sig_ref, qc_ref, adj_ref, cost_ref,
                  late_ref, cells, table, modelled, grads, where_row, where_lane, sem):
    f32 = jnp.float32
    copy = pltpu.make_async_copy(cases_hbm.at[:, EARLY:, :], late_ref, sem)
    copy.start()
    cells[...] = jnp.zeros_like(cells)

    def forward(blk, start, width):
        if start < EARLY:
            rows = early_ref[:, start:start + width, :].reshape(8 * width, 256)
        else:
            rows = late_ref[:, start - EARLY:start - EARLY + width, :].reshape(8 * width, 256)
        prod = jnp.dot(rows, f_ref[:, start:start + width], preferred_element_type=f32)
        same = lax.broadcasted_iota(jnp.int32, (width, width), 0) == lax.broadcasted_iota(
            jnp.int32, (width, width), 1)
        for k in range(8):
            one = jnp.where(same, prod[k * width:(k + 1) * width], 0.0)
            row = jnp.sum(one, axis=0, keepdims=True)
            at = k % LEV * BLOCKS + blk
            cells[k // LEV, at:at + 1, 0:width] = row

    for blk in range(BLOCKS):
        if blk * 128 == EARLY:
            copy.wait()
        forward(blk, blk * 128, min(128, PIECE - blk * 128))

    index = idx_ref[...]
    level = ((index >= PIECE).astype(jnp.int32) + (index >= 2 * PIECE).astype(jnp.int32)
             + (index >= 3 * PIECE).astype(jnp.int32))
    point = index - level * PIECE
    where_row[...] = level * BLOCKS + (point >> 7)
    where_lane[...] = point & 127

    for t in range(2):
        parts = split3(jnp.transpose(cells[t]))
        for k in range(3):
            table[t, :, k * ROWS:(k + 1) * ROWS] = parts[k]

    row_id = lax.broadcasted_iota(jnp.int32, (ROWS, CHUNK), 0)
    lane_id = lax.broadcasted_iota(jnp.int32, (128, CHUNK), 0)

    for t in range(2):
        for c in range(OBS // CHUNK):
            at = slice(c * CHUNK, (c + 1) * CHUNK)
            hot = jnp.where(row_id == where_row[t:t + 1, at], 1.0, 0.0).astype(jnp.bfloat16)
            hot = jnp.concatenate([hot, hot, hot], axis=0)
            lines = jnp.dot(table[t], hot, preferred_element_type=f32)
            lines = jnp.where(lane_id == where_lane[t:t + 1, at], lines, 0.0)
            modelled[t:t + 1, at] = jnp.sum(lines, axis=0, keepdims=True)

    sigma = sig_ref[...]
    kind = qc_ref[...]
    radius_sq = jnp.where(kind == 0, 16.0, jnp.where(kind == 1, 4.0, 1.0))
    scaled = (modelled[...] - inn_ref[...]) / sigma
    scaled_sq = scaled * scaled / radius_sq
    terms = 0.5 * radius_sq * jnp.log1p(scaled_sq)
    cost_ref[...] = jnp.broadcast_to(jnp.sum(terms, axis=(0, 1), keepdims=True), (8, 128))
    grad = scaled / ((1.0 + scaled_sq) * sigma)
    first, second, third = split3(grad)
    grads[0] = first.astype(f32)
    grads[1] = second.astype(f32)
    grads[2] = third.astype(f32)

    sums = []
    for t in range(2):
        total = jnp.zeros((3 * ROWS, 128), f32)
        for c in range(OBS // CHUNK):
            at = slice(c * CHUNK, (c + 1) * CHUNK)
            hot = row_id == where_row[t:t + 1, at]
            left = jnp.concatenate(
                [jnp.where(hot, grads[k, t:t + 1, at], 0.0).astype(jnp.bfloat16) for k in range(3)],
                axis=0)
            right = jnp.where(lane_id == where_lane[t:t + 1, at], 1.0, 0.0).astype(jnp.bfloat16)
            total = total + lax.dot_general(left, right, (((1,), (1,)), ((), ())),
                                            preferred_element_type=f32)
        sums.append(total[0:ROWS] + total[ROWS:2 * ROWS] + total[2 * ROWS:3 * ROWS])
    update = jnp.concatenate(sums, axis=0).astype(jnp.bfloat16).astype(f32)
    columns = jnp.transpose(update)

    for blk in range(BLOCKS):
        start = blk * 128
        width = min(128, PIECE - start)
        halves = []
        cols = pltpu.roll(columns, (128 - blk) % 128, axis=1)
        for half in range(width // 64):
            lanes = slice(half * 64, half * 64 + 64)
            first = start + half * 64
            held, first = (early_ref, first) if start < EARLY else (late_ref, first - EARLY)
            total = jnp.zeros((64, 256), f32)
            for k in range(8):
                j = k // LEV * ROWS + k % LEV * BLOCKS
                total = total + held[k, first:first + 64, :].astype(f32) * cols[lanes, j:j + 1]
            halves.append(total)
        total = jnp.concatenate(halves, axis=0)
        adj_ref[:, start:start + width] = jnp.transpose(total).astype(jnp.bfloat16)


def middle(early, cases, fields, obs_index, innovation, obs_sigma, qc_class):
    vm = pl.BlockSpec(memory_space=pltpu.VMEM)
    return pl.pallas_call(
        middle_kernel,
        out_shape=(jax.ShapeDtypeStruct((256, PIECE), jnp.bfloat16),
                   jax.ShapeDtypeStruct((8, 128), jnp.float32)),
        in_specs=[vm, pl.BlockSpec(memory_space=pltpu.HBM)] + [vm] * 5,
        out_specs=(vm, vm),
        scratch_shapes=[
            pltpu.VMEM((8, PIECE - EARLY, 256), jnp.bfloat16),
            pltpu.VMEM((2, ROWS, 128), jnp.float32),
            pltpu.VMEM((2, 128, 3 * ROWS), jnp.bfloat16),
            pltpu.VMEM((2, OBS), jnp.float32),
            pltpu.VMEM((3, 2, OBS), jnp.float32),
            pltpu.VMEM((2, OBS), jnp.int32),
            pltpu.VMEM((2, OBS), jnp.int32),
            pltpu.SemaphoreType.DMA,
        ],
        compiler_params=pltpu.CompilerParams(vmem_limit_bytes=40 * 1024 * 1024),
        name="middle",
    )(early, pltpu.with_memory_space_constraint(cases, pltpu.HBM), fields, obs_index, innovation,
      obs_sigma, qc_class)


F32 = jnp.float32
BF16 = jnp.bfloat16
GX = 320
GY = 160
MEMBERS = 256
WIDE = 16 * 128
SPACE = ("space_0", "space_1", "space_2")
TM = ("tm_0", "tm_1")
TM_SPACE = ("tm_0", "tm_1", "space_0", "space_1", "space_2")


def two_parts(value):
    high = np.asarray(value, np.float32).astype(ml_dtypes.bfloat16)
    low = (value - high.astype(np.float64)).astype(np.float32).astype(ml_dtypes.bfloat16)
    return high, low


def lookup_table(length):
    wave = np.arange(length)[:, None]
    angle = np.pi * (np.arange(length)[None, :] + 0.5) * wave / length
    return np.cos(angle) * np.sqrt(np.where(wave == 0, 1.0, 2.0) / length)


def split2(value):
    high = value.astype(BF16)
    return high, (value - high.astype(F32)).astype(BF16)


def product(left, right):
    (left_high, left_low), (right_high, right_low) = left, right
    return (jnp.dot(left_high, right_high, preferred_element_type=F32)
            + (jnp.dot(left_low, right_high, preferred_element_type=F32)
               + jnp.dot(left_high, right_low, preferred_element_type=F32)))


def rows_of(flat, lines, grid):
    for k in range(5):
        lines[:, k * 128:(k + 1) * 128] = flat[pl.ds(k, 80, stride=5), :]
    for k in range(4):
        grid[k * 80:(k + 1) * 80, :] = lines[:, k * GY:(k + 1) * GY]


def flat_of(grid, lines, flat):
    for k in range(4):
        lines[:, k * GY:(k + 1) * GY] = grid[k * 80:(k + 1) * 80, :]
    for k in range(5):
        flat[pl.ds(k, 80, stride=5), :] = lines[:, k * 128:(k + 1) * 128]


def first_kernel(c_hbm, s_hbm, x_hbm, y_hbm, cases_hbm, out_ref, back_ref, early_ref,
                 wide, tall, lines, grid, c_ref, s_ref, x_ref, y_ref, sems):
    pairs = ((c_hbm, c_ref), (s_hbm, s_ref), (y_hbm, y_ref), (x_hbm, x_ref), (cases_hbm.at[:, 0:EARLY, :], early_ref))
    copies = [pltpu.make_async_copy(*pair, sems.at[k]) for k, pair in enumerate(pairs)]
    for copy in copies:
        copy.start()
    wide[:, PIECE:] = jnp.zeros((32, wide.shape[1] - PIECE), F32)
    copies[0].wait()
    control = c_ref[...]
    back = 0.5 * jnp.sum(control * control, axis=(0, 1), keepdims=True)
    back_ref[...] = jnp.broadcast_to(back, (8, 128))
    copies[1].wait()
    c_ref[...] = control * s_ref[...]
    rows_of(c_ref, lines, grid)
    coeffs = split2(grid[...])
    copies[2].wait()
    rows = split2(product(coeffs, (y_ref[0], y_ref[1])))
    copies[3].wait()
    field = product((x_ref[0], x_ref[1]), rows)
    for i in range(10):
        wide[:, i * GY:(i + 1) * GY] = field[i * 32:(i + 1) * 32]
    for r in range(BLOCKS):
        tall[:, r, :] = wide[:, r * 128:(r + 1) * 128]
    for r in range(BLOCKS, 16):
        tall[:, r, :] = jnp.zeros((32, 128), F32)
    out_ref[...] = tall[...].astype(BF16)
    copies[4].wait()


def spread_kernel(in_ref, out_ref, tall, wide):
    tall[...] = in_ref[...].astype(F32)
    for r in range(BLOCKS):
        wide[:, r * 128:(r + 1) * 128] = tall[:, r, :]
    value = wide[:, 0:PIECE].astype(BF16)
    for k in range(8):
        out_ref[k] = value


def fold_kernel(in_ref, out_ref, tall, wide):
    total = in_ref[0].astype(F32)
    for k in range(1, 8):
        total = total + in_ref[k].astype(F32)
    wide[:, 0:PIECE] = total
    wide[:, PIECE:] = jnp.zeros((32, wide.shape[1] - PIECE), F32)
    for r in range(BLOCKS):
        tall[:, r, :] = wide[:, r * 128:(r + 1) * 128]
    for r in range(BLOCKS, 16):
        tall[:, r, :] = jnp.zeros((32, 128), F32)
    out_ref[...] = tall[...].astype(BF16)


def last_kernel(in_ref, c_ref, s_ref, xh, xl, yh, yl, back_ref, obs_ref, grad_ref, pay_ref,
                tall, wide, adj, lines, grid):
    tall[...] = in_ref[...].astype(F32)
    for r in range(BLOCKS):
        wide[:, r * 128:(r + 1) * 128] = tall[:, r, :]
    for i in range(10):
        adj[i * 32:(i + 1) * 32, :] = wide[:, i * GY:(i + 1) * GY].astype(BF16)
    part = adj[...]
    rows = (jnp.dot(xh[...], part, preferred_element_type=F32)
            + jnp.dot(xl[...], part, preferred_element_type=F32))
    grid[...] = product(split2(rows), (yh[...], yl[...]))
    flat_of(grid, lines, grad_ref)
    grad = c_ref[...] + s_ref[...] * grad_ref[...]
    grad_ref[...] = grad
    cost = back_ref[0:1, 0:1] + obs_ref[0:1, 0:1]
    norm = jnp.sum(grad * grad, axis=(0, 1), keepdims=True)
    lane = lax.broadcasted_iota(jnp.int32, (MEMBERS, 128), 1)
    pay_ref[...] = jnp.where(lane == 0, cost, jnp.where(lane == 1, norm, 0.0))


def step_kernel(pay_ref, c_ref, g_ref, out_ref, cost_ref):
    sums = jnp.sum(pay_ref[...], axis=0, keepdims=True)
    cost = sums[:, 0:1]
    size = 0.5 * cost / (sums[:, 1:2] + 1e-06)
    out_ref[...] = c_ref[...] - size * g_ref[...]
    cost_ref[...] = cost


def call(kernel, outs, scratch, name, specs=None):
    vm = pl.BlockSpec(memory_space=pltpu.VMEM)

    def run(*args):
        ins = [vm] * len(args)
        for at in specs or ():
            ins[at] = pl.BlockSpec(memory_space=pltpu.HBM)
        return pl.pallas_call(
            kernel,
            out_shape=tuple(jax.ShapeDtypeStruct(*out) for out in outs),
            in_specs=ins,
            out_specs=(vm,) * len(outs),
            scratch_shapes=scratch,
            compiler_params=pltpu.CompilerParams(vmem_limit_bytes=40 * 1024 * 1024),
            name=name,
        )(*args)

    return run


def exchanged(value, axis):
    return lax.all_to_all(value, axis, split_axis=0, concat_axis=0, tiled=True)


def per_device(control, spectrum, perturb, obs_index, innovation, obs_sigma, qc_class):
    waves = np.arange(GX).reshape(80, 4).T.reshape(-1)
    points = np.arange(GX).reshape(32, 10).T.reshape(-1)
    table_x = lookup_table(GX)[waves][:, points]
    table_y = lookup_table(GY)
    cases = perturb.transpose(0, 2, 3, 1).reshape(2 * LEV, PIECE, MEMBERS)
    control_flat = control.reshape(400, 128)
    spectrum_flat = spectrum.reshape(400, 128)
    tall = pltpu.VMEM((32, 16, 128), F32)
    wide = pltpu.VMEM((32, BLOCKS * 128), F32)
    lines = pltpu.VMEM((80, 640), F32)
    grid = pltpu.VMEM((GX, GY), F32)
    flat = pltpu.VMEM((400, 128), F32)

    inputs = (control_flat, spectrum_flat, jnp.asarray(np.stack(two_parts(table_x.T))),
              jnp.asarray(np.stack(two_parts(table_y))), cases)
    sent, back, early = call(
        first_kernel,
        (((32, 16, 128), BF16), ((8, 128), F32), ((2 * LEV, EARLY, MEMBERS), BF16)),
        [wide, tall, lines, grid, flat, flat, pltpu.VMEM((2, GX, GX), BF16),
         pltpu.VMEM((2, GY, GY), BF16), pltpu.SemaphoreType.DMA((5,))],
        "synthesis", specs=range(5),
    )(*[pltpu.with_memory_space_constraint(value, pltpu.HBM) for value in inputs])
    pieces = exchanged(sent, SPACE)
    (copies,) = call(spread_kernel, (((8, 32, PIECE), BF16),), [tall, wide], "spread")(pieces)
    fields = exchanged(copies, TM).reshape(MEMBERS, PIECE)
    partial, obs = middle(early, cases, fields, obs_index, innovation, obs_sigma, qc_class)
    terms = exchanged(partial.reshape(8, 32, PIECE), TM)
    (summed,) = call(fold_kernel, (((32, 16, 128), BF16),), [tall, wide], "fold")(terms)
    adjoint = exchanged(summed, SPACE)
    gradient, mine = call(
        last_kernel,
        (((400, 128), F32), ((MEMBERS, 128), F32)),
        [tall, wide, pltpu.VMEM((GX, GY), BF16), lines, grid],
        "analysis",
    )(adjoint, control_flat, spectrum_flat, *two_parts(table_x), *two_parts(table_y.T), back, obs)
    sums = exchanged(mine.reshape(MEMBERS, 1, 128), TM_SPACE).reshape(MEMBERS, 128)
    result, cost = call(
        step_kernel, (((400, 128), F32), ((1, 1), F32)), [], "step"
    )(sums, control_flat, gradient)
    return result.reshape(1, GX * GY), cost.reshape(1)


def solution(mesh):
    split = Mesh(
        mesh.devices.reshape(2, 4, 4, 4, 2), ("tm_0", "tm_1", "space_0", "space_1", "space_2")
    )
    return jax.shard_map(
        per_device,
        mesh=split,
        in_specs=(
            P(TM_SPACE, None),
            P(),
            P(TM, None, None, SPACE),
            P(TM, SPACE),
            P(TM, SPACE),
            P(TM, SPACE),
            P(TM, SPACE),
        ),
        out_specs=(P(TM_SPACE, None), P()),
        check_vma=False,
    )
```

```python
import jax
import jax.numpy as jnp
import ml_dtypes
import numpy as np
from jax import lax
from jax.experimental import pallas as pl
from jax.experimental.pallas import tpu as pltpu
from jax.sharding import Mesh
from jax.sharding import PartitionSpec as P

PIECE = 1600
LEV = 4
BLOCKS = 13
ROWS = 64
OBS = 2048
CHUNK = 256
EARLY = 1280


def split3(value):
    first = value.astype(jnp.bfloat16)
    rest = value - first.astype(jnp.float32)
    second = rest.astype(jnp.bfloat16)
    third = (rest - second.astype(jnp.float32)).astype(jnp.bfloat16)
    return first, second, third


def middle_kernel(early_ref, cases_hbm, f_ref, idx_ref, inn_ref, sig_ref, qc_ref, adj_ref, cost_ref,
                  late_ref, cells, table, modelled, grads, where_row, where_lane, sem):
    f32 = jnp.float32
    copy = pltpu.make_async_copy(cases_hbm.at[:, EARLY:, :], late_ref, sem)
    copy.start()
    cells[...] = jnp.zeros_like(cells)

    def forward(blk, start, width):
        if start < EARLY:
            rows = early_ref[:, start:start + width, :].reshape(8 * width, 256)
        else:
            rows = late_ref[:, start - EARLY:start - EARLY + width, :].reshape(8 * width, 256)
        prod = jnp.dot(rows, f_ref[:, start:start + width], preferred_element_type=f32)
        same = lax.broadcasted_iota(jnp.int32, (width, width), 0) == lax.broadcasted_iota(
            jnp.int32, (width, width), 1)
        for k in range(8):
            one = jnp.where(same, prod[k * width:(k + 1) * width], 0.0)
            row = jnp.sum(one, axis=0, keepdims=True)
            at = k % LEV * BLOCKS + blk
            cells[k // LEV, at:at + 1, 0:width] = row

    for blk in range(BLOCKS):
        if blk * 128 == EARLY:
            copy.wait()
        forward(blk, blk * 128, min(128, PIECE - blk * 128))

    index = idx_ref[...]
    level = ((index >= PIECE).astype(jnp.int32) + (index >= 2 * PIECE).astype(jnp.int32)
             + (index >= 3 * PIECE).astype(jnp.int32))
    point = index - level * PIECE
    where_row[...] = level * BLOCKS + (point >> 7)
    where_lane[...] = point & 127

    for t in range(2):
        parts = split3(jnp.transpose(cells[t]))
        for k in range(3):
            table[t, :, k * ROWS:(k + 1) * ROWS] = parts[k]

    row_id = lax.broadcasted_iota(jnp.int32, (ROWS, CHUNK), 0)
    lane_id = lax.broadcasted_iota(jnp.int32, (128, CHUNK), 0)

    for t in range(2):
        for c in range(OBS // CHUNK):
            at = slice(c * CHUNK, (c + 1) * CHUNK)
            hot = jnp.where(row_id == where_row[t:t + 1, at], 1.0, 0.0).astype(jnp.bfloat16)
            hot = jnp.concatenate([hot, hot, hot], axis=0)
            lines = jnp.dot(table[t], hot, preferred_element_type=f32)
            lines = jnp.where(lane_id == where_lane[t:t + 1, at], lines, 0.0)
            modelled[t:t + 1, at] = jnp.sum(lines, axis=0, keepdims=True)

    sigma = sig_ref[...]
    kind = qc_ref[...]
    radius_sq = jnp.where(kind == 0, 16.0, jnp.where(kind == 1, 4.0, 1.0))
    scaled = (modelled[...] - inn_ref[...]) / sigma
    scaled_sq = scaled * scaled / radius_sq
    terms = 0.5 * radius_sq * jnp.log1p(scaled_sq)
    cost_ref[...] = jnp.broadcast_to(jnp.sum(terms, axis=(0, 1), keepdims=True), (8, 128))
    grad = scaled / ((1.0 + scaled_sq) * sigma)
    first, second, third = split3(grad)
    grads[0] = first.astype(f32)
    grads[1] = second.astype(f32)
    grads[2] = third.astype(f32)

    sums = []
    for t in range(2):
        total = jnp.zeros((3 * ROWS, 128), f32)
        for c in range(OBS // CHUNK):
            at = slice(c * CHUNK, (c + 1) * CHUNK)
            hot = row_id == where_row[t:t + 1, at]
            left = jnp.concatenate(
                [jnp.where(hot, grads[k, t:t + 1, at], 0.0).astype(jnp.bfloat16) for k in range(3)],
                axis=0)
            right = jnp.where(lane_id == where_lane[t:t + 1, at], 1.0, 0.0).astype(jnp.bfloat16)
            total = total + lax.dot_general(left, right, (((1,), (1,)), ((), ())),
                                            preferred_element_type=f32)
        sums.append(total[0:ROWS] + total[ROWS:2 * ROWS] + total[2 * ROWS:3 * ROWS])
    update = jnp.concatenate(sums, axis=0).astype(jnp.bfloat16).astype(f32)
    columns = jnp.transpose(update)
    same = lax.broadcasted_iota(jnp.int32, (128, 128), 0) == lax.broadcasted_iota(
        jnp.int32, (128, 128), 1)

    for blk in range(BLOCKS):
        start = blk * 128
        width = min(128, PIECE - start)
        held, first = (early_ref, start) if start < EARLY else (late_ref, start - EARLY)
        if blk % 3 != 0 and width == 128:
            diagonals = []
            for k in range(8):
                j = k // LEV * ROWS + k % LEV * BLOCKS + blk
                diagonals.append(jnp.where(same, update[j:j + 1], 0.0).astype(jnp.bfloat16))
            total = jnp.dot(jnp.concatenate(diagonals, axis=1),
                            held[:, first:first + width, :].reshape(8 * width, 256),
                            preferred_element_type=f32)
        else:
            cols = pltpu.roll(columns, (128 - blk) % 128, axis=1)
            halves = []
            for half in range(width // 64):
                lanes = slice(half * 64, half * 64 + 64)
                here = first + half * 64
                total = jnp.zeros((64, 256), f32)
                for k in range(8):
                    j = k // LEV * ROWS + k % LEV * BLOCKS
                    total = total + held[k, here:here + 64, :].astype(f32) * cols[lanes, j:j + 1]
                halves.append(total)
            total = jnp.concatenate(halves, axis=0)
        adj_ref[:, start:start + width] = jnp.transpose(total).astype(jnp.bfloat16)


def middle(early, cases, fields, obs_index, innovation, obs_sigma, qc_class):
    vm = pl.BlockSpec(memory_space=pltpu.VMEM)
    return pl.pallas_call(
        middle_kernel,
        out_shape=(jax.ShapeDtypeStruct((256, PIECE), jnp.bfloat16),
                   jax.ShapeDtypeStruct((8, 128), jnp.float32)),
        in_specs=[vm, pl.BlockSpec(memory_space=pltpu.HBM)] + [vm] * 5,
        out_specs=(vm, vm),
        scratch_shapes=[
            pltpu.VMEM((8, PIECE - EARLY, 256), jnp.bfloat16),
            pltpu.VMEM((2, ROWS, 128), jnp.float32),
            pltpu.VMEM((2, 128, 3 * ROWS), jnp.bfloat16),
            pltpu.VMEM((2, OBS), jnp.float32),
            pltpu.VMEM((3, 2, OBS), jnp.float32),
            pltpu.VMEM((2, OBS), jnp.int32),
            pltpu.VMEM((2, OBS), jnp.int32),
            pltpu.SemaphoreType.DMA,
        ],
        compiler_params=pltpu.CompilerParams(vmem_limit_bytes=40 * 1024 * 1024),
        name="middle",
    )(early, pltpu.with_memory_space_constraint(cases, pltpu.HBM), fields, obs_index, innovation,
      obs_sigma, qc_class)


F32 = jnp.float32
BF16 = jnp.bfloat16
GX = 320
GY = 160
MEMBERS = 256
WIDE = 16 * 128
SPACE = ("space_0", "space_1", "space_2")
TM = ("tm_0", "tm_1")
TM_SPACE = ("tm_0", "tm_1", "space_0", "space_1", "space_2")


def two_parts(value):
    high = np.asarray(value, np.float32).astype(ml_dtypes.bfloat16)
    low = (value - high.astype(np.float64)).astype(np.float32).astype(ml_dtypes.bfloat16)
    return high, low


def lookup_table(length):
    wave = np.arange(length)[:, None]
    angle = np.pi * (np.arange(length)[None, :] + 0.5) * wave / length
    return np.cos(angle) * np.sqrt(np.where(wave == 0, 1.0, 2.0) / length)


def split2(value):
    high = value.astype(BF16)
    return high, (value - high.astype(F32)).astype(BF16)


def product(left, right):
    (left_high, left_low), (right_high, right_low) = left, right
    return (jnp.dot(left_high, right_high, preferred_element_type=F32)
            + (jnp.dot(left_low, right_high, preferred_element_type=F32)
               + jnp.dot(left_high, right_low, preferred_element_type=F32)))


def rows_of(flat, lines, grid):
    for k in range(5):
        lines[:, k * 128:(k + 1) * 128] = flat[pl.ds(k, 80, stride=5), :]
    for k in range(4):
        grid[k * 80:(k + 1) * 80, :] = lines[:, k * GY:(k + 1) * GY]


def flat_of(grid, lines, flat):
    for k in range(4):
        lines[:, k * GY:(k + 1) * GY] = grid[k * 80:(k + 1) * 80, :]
    for k in range(5):
        flat[pl.ds(k, 80, stride=5), :] = lines[:, k * 128:(k + 1) * 128]


def first_kernel(c_hbm, s_hbm, x_hbm, y_hbm, cases_hbm, out_ref, back_ref, early_ref,
                 wide, tall, lines, grid, c_ref, s_ref, x_ref, y_ref, sems):
    pairs = ((c_hbm, c_ref), (s_hbm, s_ref), (y_hbm, y_ref), (x_hbm, x_ref), (cases_hbm.at[:, 0:EARLY, :], early_ref))
    copies = [pltpu.make_async_copy(*pair, sems.at[k]) for k, pair in enumerate(pairs)]
    for copy in copies:
        copy.start()
    wide[:, PIECE:] = jnp.zeros((32, wide.shape[1] - PIECE), F32)
    copies[0].wait()
    control = c_ref[...]
    back = 0.5 * jnp.sum(control * control, axis=(0, 1), keepdims=True)
    back_ref[...] = jnp.broadcast_to(back, (8, 128))
    copies[1].wait()
    c_ref[...] = control * s_ref[...]
    rows_of(c_ref, lines, grid)
    coeffs = split2(grid[...])
    copies[2].wait()
    rows = split2(product(coeffs, (y_ref[0], y_ref[1])))
    copies[3].wait()
    field = product((x_ref[0], x_ref[1]), rows)
    for i in range(10):
        wide[:, i * GY:(i + 1) * GY] = field[i * 32:(i + 1) * 32]
    for r in range(BLOCKS):
        tall[:, r, :] = wide[:, r * 128:(r + 1) * 128]
    for r in range(BLOCKS, 16):
        tall[:, r, :] = jnp.zeros((32, 128), F32)
    out_ref[...] = tall[...].astype(BF16)
    copies[4].wait()


def spread_kernel(in_ref, out_ref, tall, wide):
    tall[...] = in_ref[...].astype(F32)
    for r in range(BLOCKS):
        wide[:, r * 128:(r + 1) * 128] = tall[:, r, :]
    value = wide[:, 0:PIECE].astype(BF16)
    for k in range(8):
        out_ref[k] = value


def fold_kernel(in_ref, out_ref, tall, wide):
    total = in_ref[0].astype(F32)
    for k in range(1, 8):
        total = total + in_ref[k].astype(F32)
    wide[:, 0:PIECE] = total
    wide[:, PIECE:] = jnp.zeros((32, wide.shape[1] - PIECE), F32)
    for r in range(BLOCKS):
        tall[:, r, :] = wide[:, r * 128:(r + 1) * 128]
    for r in range(BLOCKS, 16):
        tall[:, r, :] = jnp.zeros((32, 128), F32)
    out_ref[...] = tall[...].astype(BF16)


def last_kernel(in_ref, c_ref, s_ref, xh, xl, yh, yl, back_ref, obs_ref, grad_ref, pay_ref,
                tall, wide, adj, lines, grid):
    tall[...] = in_ref[...].astype(F32)
    for r in range(BLOCKS):
        wide[:, r * 128:(r + 1) * 128] = tall[:, r, :]
    for i in range(10):
        adj[i * 32:(i + 1) * 32, :] = wide[:, i * GY:(i + 1) * GY].astype(BF16)
    part = adj[...]
    rows = (jnp.dot(xh[...], part, preferred_element_type=F32)
            + jnp.dot(xl[...], part, preferred_element_type=F32))
    grid[...] = product(split2(rows), (yh[...], yl[...]))
    flat_of(grid, lines, grad_ref)
    grad = c_ref[...] + s_ref[...] * grad_ref[...]
    grad_ref[...] = grad
    cost = back_ref[0:1, 0:1] + obs_ref[0:1, 0:1]
    norm = jnp.sum(grad * grad, axis=(0, 1), keepdims=True)
    lane = lax.broadcasted_iota(jnp.int32, (MEMBERS, 128), 1)
    pay_ref[...] = jnp.where(lane == 0, cost, jnp.where(lane == 1, norm, 0.0))


def step_kernel(pay_ref, c_ref, g_ref, out_ref, cost_ref):
    sums = jnp.sum(pay_ref[...], axis=0, keepdims=True)
    cost = sums[:, 0:1]
    size = 0.5 * cost / (sums[:, 1:2] + 1e-06)
    out_ref[...] = c_ref[...] - size * g_ref[...]
    cost_ref[...] = cost


def call(kernel, outs, scratch, name, specs=None):
    vm = pl.BlockSpec(memory_space=pltpu.VMEM)

    def run(*args):
        ins = [vm] * len(args)
        for at in specs or ():
            ins[at] = pl.BlockSpec(memory_space=pltpu.HBM)
        return pl.pallas_call(
            kernel,
            out_shape=tuple(jax.ShapeDtypeStruct(*out) for out in outs),
            in_specs=ins,
            out_specs=(vm,) * len(outs),
            scratch_shapes=scratch,
            compiler_params=pltpu.CompilerParams(vmem_limit_bytes=40 * 1024 * 1024),
            name=name,
        )(*args)

    return run


def exchanged(value, axis):
    return lax.all_to_all(value, axis, split_axis=0, concat_axis=0, tiled=True)


def per_device(control, spectrum, perturb, obs_index, innovation, obs_sigma, qc_class):
    waves = np.arange(GX).reshape(80, 4).T.reshape(-1)
    points = np.arange(GX).reshape(32, 10).T.reshape(-1)
    table_x = lookup_table(GX)[waves][:, points]
    table_y = lookup_table(GY)
    cases = perturb.transpose(0, 2, 3, 1).reshape(2 * LEV, PIECE, MEMBERS)
    control_flat = control.reshape(400, 128)
    spectrum_flat = spectrum.reshape(400, 128)
    tall = pltpu.VMEM((32, 16, 128), F32)
    wide = pltpu.VMEM((32, BLOCKS * 128), F32)
    lines = pltpu.VMEM((80, 640), F32)
    grid = pltpu.VMEM((GX, GY), F32)
    flat = pltpu.VMEM((400, 128), F32)

    inputs = (control_flat, spectrum_flat, jnp.asarray(np.stack(two_parts(table_x.T))),
              jnp.asarray(np.stack(two_parts(table_y))), cases)
    sent, back, early = call(
        first_kernel,
        (((32, 16, 128), BF16), ((8, 128), F32), ((2 * LEV, EARLY, MEMBERS), BF16)),
        [wide, tall, lines, grid, flat, flat, pltpu.VMEM((2, GX, GX), BF16),
         pltpu.VMEM((2, GY, GY), BF16), pltpu.SemaphoreType.DMA((5,))],
        "synthesis", specs=range(5),
    )(*[pltpu.with_memory_space_constraint(value, pltpu.HBM) for value in inputs])
    pieces = exchanged(sent, SPACE)
    (copies,) = call(spread_kernel, (((8, 32, PIECE), BF16),), [tall, wide], "spread")(pieces)
    fields = exchanged(copies, TM).reshape(MEMBERS, PIECE)
    partial, obs = middle(early, cases, fields, obs_index, innovation, obs_sigma, qc_class)
    terms = exchanged(partial.reshape(8, 32, PIECE), TM)
    (summed,) = call(fold_kernel, (((32, 16, 128), BF16),), [tall, wide], "fold")(terms)
    adjoint = exchanged(summed, SPACE)
    gradient, mine = call(
        last_kernel,
        (((400, 128), F32), ((MEMBERS, 128), F32)),
        [tall, wide, pltpu.VMEM((GX, GY), BF16), lines, grid],
        "analysis",
    )(adjoint, control_flat, spectrum_flat, *two_parts(table_x), *two_parts(table_y.T), back, obs)
    sums = exchanged(mine.reshape(MEMBERS, 1, 128), TM_SPACE).reshape(MEMBERS, 128)
    result, cost = call(
        step_kernel, (((400, 128), F32), ((1, 1), F32)), [], "step"
    )(sums, control_flat, gradient)
    return result.reshape(1, GX * GY), cost.reshape(1)


def solution(mesh):
    split = Mesh(
        mesh.devices.reshape(2, 4, 4, 4, 2), ("tm_0", "tm_1", "space_0", "space_1", "space_2")
    )
    return jax.shard_map(
        per_device,
        mesh=split,
        in_specs=(
            P(TM_SPACE, None),
            P(),
            P(TM, None, None, SPACE),
            P(TM, SPACE),
            P(TM, SPACE),
            P(TM, SPACE),
            P(TM, SPACE),
        ),
        out_specs=(P(TM_SPACE, None), P()),
        check_vma=False,
    )
```

```python
import jax
import jax.numpy as jnp
import ml_dtypes
import numpy as np
from jax import lax
from jax.experimental import pallas as pl
from jax.experimental.pallas import tpu as pltpu
from jax.sharding import Mesh
from jax.sharding import PartitionSpec as P

PIECE = 1600
LEV = 4
BLOCKS = 13
ROWS = 64
OBS = 2048
CHUNK = 256
EARLY = 1280


def split3(value):
    first = value.astype(jnp.bfloat16)
    rest = value - first.astype(jnp.float32)
    second = rest.astype(jnp.bfloat16)
    third = (rest - second.astype(jnp.float32)).astype(jnp.bfloat16)
    return first, second, third


def middle_kernel(early_ref, cases_hbm, f_ref, idx_ref, inn_ref, sig_ref, qc_ref, adj_ref, cost_ref,
                  late_ref, cells, table, modelled, grads, where_row, where_lane, sem):
    f32 = jnp.float32
    copy = pltpu.make_async_copy(cases_hbm.at[:, EARLY:, :], late_ref, sem)
    copy.start()
    cells[...] = jnp.zeros_like(cells)

    def forward(blk, start, width):
        if start < EARLY:
            rows = early_ref[:, start:start + width, :].reshape(8 * width, 256)
        else:
            rows = late_ref[:, start - EARLY:start - EARLY + width, :].reshape(8 * width, 256)
        if width == 128:
            fields = f_ref[:, blk * 32:(blk + 1) * 32, :].reshape(256, 128)
        else:
            tail = f_ref[:, 384:400, :].astype(f32)
            tail = jnp.concatenate([tail, pltpu.roll(tail, 64, axis=2)], axis=1)
            fields = tail.reshape(256, 128)[:, 0:64].astype(jnp.bfloat16)
        prod = jnp.dot(rows, fields, preferred_element_type=f32)
        same = lax.broadcasted_iota(jnp.int32, (width, width), 0) == lax.broadcasted_iota(
            jnp.int32, (width, width), 1)
        for k in range(8):
            one = jnp.where(same, prod[k * width:(k + 1) * width], 0.0)
            row = jnp.sum(one, axis=0, keepdims=True)
            at = k % LEV * BLOCKS + blk
            cells[k // LEV, at:at + 1, 0:width] = row

    for blk in range(BLOCKS):
        if blk * 128 == EARLY:
            copy.wait()
        forward(blk, blk * 128, min(128, PIECE - blk * 128))

    index = idx_ref[...]
    level = ((index >= PIECE).astype(jnp.int32) + (index >= 2 * PIECE).astype(jnp.int32)
             + (index >= 3 * PIECE).astype(jnp.int32))
    point = index - level * PIECE
    where_row[...] = level * BLOCKS + (point >> 7)
    where_lane[...] = point & 127

    for t in range(2):
        parts = split3(jnp.transpose(cells[t]))
        for k in range(3):
            table[t, :, k * ROWS:(k + 1) * ROWS] = parts[k]

    row_id = lax.broadcasted_iota(jnp.int32, (ROWS, CHUNK), 0)
    lane_id = lax.broadcasted_iota(jnp.int32, (128, CHUNK), 0)

    for t in range(2):
        for c in range(OBS // CHUNK):
            at = slice(c * CHUNK, (c + 1) * CHUNK)
            hot = jnp.where(row_id == where_row[t:t + 1, at], 1.0, 0.0).astype(jnp.bfloat16)
            hot = jnp.concatenate([hot, hot, hot], axis=0)
            lines = jnp.dot(table[t], hot, preferred_element_type=f32)
            lines = jnp.where(lane_id == where_lane[t:t + 1, at], lines, 0.0)
            modelled[t:t + 1, at] = jnp.sum(lines, axis=0, keepdims=True)

    sigma = sig_ref[...]
    kind = qc_ref[...]
    radius_sq = jnp.where(kind == 0, 16.0, jnp.where(kind == 1, 4.0, 1.0))
    scaled = (modelled[...] - inn_ref[...]) / sigma
    scaled_sq = scaled * scaled / radius_sq
    terms = 0.5 * radius_sq * jnp.log1p(scaled_sq)
    cost_ref[...] = jnp.broadcast_to(jnp.sum(terms, axis=(0, 1), keepdims=True), (8, 128))
    grad = scaled / ((1.0 + scaled_sq) * sigma)
    first, second, third = split3(grad)
    grads[0] = first.astype(f32)
    grads[1] = second.astype(f32)
    grads[2] = third.astype(f32)

    sums = []
    for t in range(2):
        total = jnp.zeros((3 * ROWS, 128), f32)
        for c in range(OBS // CHUNK):
            at = slice(c * CHUNK, (c + 1) * CHUNK)
            hot = row_id == where_row[t:t + 1, at]
            left = jnp.concatenate(
                [jnp.where(hot, grads[k, t:t + 1, at], 0.0).astype(jnp.bfloat16) for k in range(3)],
                axis=0)
            right = jnp.where(lane_id == where_lane[t:t + 1, at], 1.0, 0.0).astype(jnp.bfloat16)
            total = total + lax.dot_general(left, right, (((1,), (1,)), ((), ())),
                                            preferred_element_type=f32)
        sums.append(total[0:ROWS] + total[ROWS:2 * ROWS] + total[2 * ROWS:3 * ROWS])
    update = jnp.concatenate(sums, axis=0).astype(jnp.bfloat16).astype(f32)
    columns = jnp.transpose(update)
    same = lax.broadcasted_iota(jnp.int32, (128, 128), 0) == lax.broadcasted_iota(
        jnp.int32, (128, 128), 1)

    for blk in range(BLOCKS):
        start = blk * 128
        width = min(128, PIECE - start)
        held, first = (early_ref, start) if start < EARLY else (late_ref, start - EARLY)
        if blk % 3 != 0 and width == 128:
            diagonals = []
            for k in range(8):
                j = k // LEV * ROWS + k % LEV * BLOCKS + blk
                diagonals.append(jnp.where(same, update[j:j + 1], 0.0).astype(jnp.bfloat16))
            total = jnp.dot(jnp.concatenate(diagonals, axis=1),
                            held[:, first:first + width, :].reshape(8 * width, 256),
                            preferred_element_type=f32)
        else:
            cols = pltpu.roll(columns, (128 - blk) % 128, axis=1)
            halves = []
            for half in range(width // 64):
                lanes = slice(half * 64, half * 64 + 64)
                here = first + half * 64
                total = jnp.zeros((64, 256), f32)
                for k in range(8):
                    j = k // LEV * ROWS + k % LEV * BLOCKS
                    total = total + held[k, here:here + 64, :].astype(f32) * cols[lanes, j:j + 1]
                halves.append(total)
            total = jnp.concatenate(halves, axis=0)
        total = jnp.transpose(total)
        if width == 128:
            adj_ref[:, blk * 32:(blk + 1) * 32, :] = total.astype(jnp.bfloat16).reshape(8, 32, 128)
        else:
            total = total.reshape(8, 32, 64)
            total = jnp.concatenate([total[:, 0:16], total[:, 16:32]], axis=2)
            adj_ref[:, 384:400, :] = total.astype(jnp.bfloat16)


def middle(early, cases, fields, obs_index, innovation, obs_sigma, qc_class):
    vm = pl.BlockSpec(memory_space=pltpu.VMEM)
    return pl.pallas_call(
        middle_kernel,
        out_shape=(jax.ShapeDtypeStruct((8, 400, 128), jnp.bfloat16),
                   jax.ShapeDtypeStruct((8, 128), jnp.float32)),
        in_specs=[vm, pl.BlockSpec(memory_space=pltpu.HBM)] + [vm] * 5,
        out_specs=(vm, vm),
        scratch_shapes=[
            pltpu.VMEM((8, PIECE - EARLY, 256), jnp.bfloat16),
            pltpu.VMEM((2, ROWS, 128), jnp.float32),
            pltpu.VMEM((2, 128, 3 * ROWS), jnp.bfloat16),
            pltpu.VMEM((2, OBS), jnp.float32),
            pltpu.VMEM((3, 2, OBS), jnp.float32),
            pltpu.VMEM((2, OBS), jnp.int32),
            pltpu.VMEM((2, OBS), jnp.int32),
            pltpu.SemaphoreType.DMA,
        ],
        compiler_params=pltpu.CompilerParams(vmem_limit_bytes=40 * 1024 * 1024),
        name="middle",
    )(early, pltpu.with_memory_space_constraint(cases, pltpu.HBM), fields, obs_index, innovation,
      obs_sigma, qc_class)


F32 = jnp.float32
BF16 = jnp.bfloat16
GX = 320
GY = 160
MEMBERS = 256
WIDE = 16 * 128
SPACE = ("space_0", "space_1", "space_2")
TM = ("tm_0", "tm_1")
TM_SPACE = ("tm_0", "tm_1", "space_0", "space_1", "space_2")


def two_parts(value):
    high = np.asarray(value, np.float32).astype(ml_dtypes.bfloat16)
    low = (value - high.astype(np.float64)).astype(np.float32).astype(ml_dtypes.bfloat16)
    return high, low


def lookup_table(length):
    wave = np.arange(length)[:, None]
    angle = np.pi * (np.arange(length)[None, :] + 0.5) * wave / length
    return np.cos(angle) * np.sqrt(np.where(wave == 0, 1.0, 2.0) / length)


def split2(value):
    high = value.astype(BF16)
    return high, (value - high.astype(F32)).astype(BF16)


def product(left, right):
    (left_high, left_low), (right_high, right_low) = left, right
    return (jnp.dot(left_high, right_high, preferred_element_type=F32)
            + (jnp.dot(left_low, right_high, preferred_element_type=F32)
               + jnp.dot(left_high, right_low, preferred_element_type=F32)))


def rows_of(flat, lines, grid):
    for k in range(5):
        lines[:, k * 128:(k + 1) * 128] = flat[pl.ds(k, 80, stride=5), :]
    for k in range(4):
        grid[k * 80:(k + 1) * 80, :] = lines[:, k * GY:(k + 1) * GY]


def flat_of(grid, lines, flat):
    for k in range(4):
        lines[:, k * GY:(k + 1) * GY] = grid[k * 80:(k + 1) * 80, :]
    for k in range(5):
        flat[pl.ds(k, 80, stride=5), :] = lines[:, k * 128:(k + 1) * 128]


def first_kernel(c_hbm, s_hbm, x_hbm, y_hbm, cases_hbm, out_ref, back_ref, early_ref,
                 wide, tall, lines, grid, c_ref, s_ref, x_ref, y_ref, sems):
    pairs = ((c_hbm, c_ref), (s_hbm, s_ref), (y_hbm, y_ref), (x_hbm, x_ref), (cases_hbm.at[:, 0:EARLY, :], early_ref))
    copies = [pltpu.make_async_copy(*pair, sems.at[k]) for k, pair in enumerate(pairs)]
    for copy in copies:
        copy.start()
    wide[:, PIECE:] = jnp.zeros((32, wide.shape[1] - PIECE), F32)
    copies[0].wait()
    control = c_ref[...]
    back = 0.5 * jnp.sum(control * control, axis=(0, 1), keepdims=True)
    back_ref[...] = jnp.broadcast_to(back, (8, 128))
    copies[1].wait()
    c_ref[...] = control * s_ref[...]
    rows_of(c_ref, lines, grid)
    coeffs = split2(grid[...])
    copies[2].wait()
    rows = split2(product(coeffs, (y_ref[0], y_ref[1])))
    copies[3].wait()
    field = product((x_ref[0], x_ref[1]), rows)
    for i in range(10):
        wide[:, i * GY:(i + 1) * GY] = field[i * 32:(i + 1) * 32]
    for r in range(BLOCKS):
        tall[:, r, :] = wide[:, r * 128:(r + 1) * 128]
    for r in range(BLOCKS, 16):
        tall[:, r, :] = jnp.zeros((32, 128), F32)
    out_ref[...] = tall[...].astype(BF16)
    copies[4].wait()


def spread_kernel(in_ref, out_ref, tall, lines):
    tall[...] = in_ref[...].astype(F32)
    for r in range(12):
        lines[r * 32:(r + 1) * 32, :] = tall[:, r, :]
    tail = tall[:, 12, :]
    lane = lax.broadcasted_iota(jnp.int32, (16, 128), 1)
    lines[384:400, :] = jnp.where(lane < 64, tail[0:16], pltpu.roll(tail[16:32], 64, axis=1))
    value = lines[...].astype(BF16)
    for k in range(8):
        out_ref[k] = value


def fold_kernel(in_ref, out_ref, tall):
    total = in_ref[0].astype(F32)
    for k in range(1, 8):
        total = total + in_ref[k].astype(F32)
    for r in range(12):
        tall[:, r, :] = total[r * 32:(r + 1) * 32]
    tail = total[384:400]
    tall[:, 12, :] = jnp.concatenate([tail, pltpu.roll(tail, 64, axis=1)], axis=0)
    for r in range(BLOCKS, 16):
        tall[:, r, :] = jnp.zeros((32, 128), F32)
    out_ref[...] = tall[...].astype(BF16)


def last_kernel(in_ref, c_ref, s_ref, xh, xl, yh, yl, back_ref, obs_ref, grad_ref, pay_ref,
                tall, wide, adj, lines, grid):
    tall[...] = in_ref[...].astype(F32)
    for r in range(BLOCKS):
        wide[:, r * 128:(r + 1) * 128] = tall[:, r, :]
    for i in range(10):
        adj[i * 32:(i + 1) * 32, :] = wide[:, i * GY:(i + 1) * GY].astype(BF16)
    part = adj[...]
    rows = (jnp.dot(xh[...], part, preferred_element_type=F32)
            + jnp.dot(xl[...], part, preferred_element_type=F32))
    grid[...] = product(split2(rows), (yh[...], yl[...]))
    flat_of(grid, lines, grad_ref)
    grad = c_ref[...] + s_ref[...] * grad_ref[...]
    grad_ref[...] = grad
    cost = back_ref[0:1, 0:1] + obs_ref[0:1, 0:1]
    norm = jnp.sum(grad * grad, axis=(0, 1), keepdims=True)
    lane = lax.broadcasted_iota(jnp.int32, (MEMBERS, 128), 1)
    pay_ref[...] = jnp.where(lane == 0, cost, jnp.where(lane == 1, norm, 0.0))


def step_kernel(pay_ref, c_ref, g_ref, out_ref, cost_ref):
    sums = jnp.sum(pay_ref[...], axis=0, keepdims=True)
    cost = sums[:, 0:1]
    size = 0.5 * cost / (sums[:, 1:2] + 1e-06)
    out_ref[...] = c_ref[...] - size * g_ref[...]
    cost_ref[...] = cost


def call(kernel, outs, scratch, name, specs=None):
    vm = pl.BlockSpec(memory_space=pltpu.VMEM)

    def run(*args):
        ins = [vm] * len(args)
        for at in specs or ():
            ins[at] = pl.BlockSpec(memory_space=pltpu.HBM)
        return pl.pallas_call(
            kernel,
            out_shape=tuple(jax.ShapeDtypeStruct(*out) for out in outs),
            in_specs=ins,
            out_specs=(vm,) * len(outs),
            scratch_shapes=scratch,
            compiler_params=pltpu.CompilerParams(vmem_limit_bytes=40 * 1024 * 1024),
            name=name,
        )(*args)

    return run


def exchanged(value, axis):
    return lax.all_to_all(value, axis, split_axis=0, concat_axis=0, tiled=True)


def per_device(control, spectrum, perturb, obs_index, innovation, obs_sigma, qc_class):
    waves = np.arange(GX).reshape(80, 4).T.reshape(-1)
    points = np.arange(GX).reshape(32, 10).T.reshape(-1)
    table_x = lookup_table(GX)[waves][:, points]
    table_y = lookup_table(GY)
    cases = perturb.transpose(0, 2, 3, 1).reshape(2 * LEV, PIECE, MEMBERS)
    control_flat = control.reshape(400, 128)
    spectrum_flat = spectrum.reshape(400, 128)
    tall = pltpu.VMEM((32, 16, 128), F32)
    wide = pltpu.VMEM((32, BLOCKS * 128), F32)
    lines = pltpu.VMEM((80, 640), F32)
    grid = pltpu.VMEM((GX, GY), F32)
    flat = pltpu.VMEM((400, 128), F32)

    inputs = (control_flat, spectrum_flat, jnp.asarray(np.stack(two_parts(table_x.T))),
              jnp.asarray(np.stack(two_parts(table_y))), cases)
    sent, back, early = call(
        first_kernel,
        (((32, 16, 128), BF16), ((8, 128), F32), ((2 * LEV, EARLY, MEMBERS), BF16)),
        [wide, tall, lines, grid, flat, flat, pltpu.VMEM((2, GX, GX), BF16),
         pltpu.VMEM((2, GY, GY), BF16), pltpu.SemaphoreType.DMA((5,))],
        "synthesis", specs=range(5),
    )(*[pltpu.with_memory_space_constraint(value, pltpu.HBM) for value in inputs])
    pieces = exchanged(sent, SPACE)
    (copies,) = call(spread_kernel, (((8, 400, 128), BF16),), [tall, flat], "spread")(pieces)
    fields = exchanged(copies, TM)
    partial, obs = middle(early, cases, fields, obs_index, innovation, obs_sigma, qc_class)
    terms = exchanged(partial, TM)
    (summed,) = call(fold_kernel, (((32, 16, 128), BF16),), [tall], "fold")(terms)
    adjoint = exchanged(summed, SPACE)
    gradient, mine = call(
        last_kernel,
        (((400, 128), F32), ((MEMBERS, 128), F32)),
        [tall, wide, pltpu.VMEM((GX, GY), BF16), lines, grid],
        "analysis",
    )(adjoint, control_flat, spectrum_flat, *two_parts(table_x), *two_parts(table_y.T), back, obs)
    sums = exchanged(mine.reshape(MEMBERS, 1, 128), TM_SPACE).reshape(MEMBERS, 128)
    result, cost = call(
        step_kernel, (((400, 128), F32), ((1, 1), F32)), [], "step"
    )(sums, control_flat, gradient)
    return result.reshape(1, GX * GY), cost.reshape(1)


def solution(mesh):
    split = Mesh(
        mesh.devices.reshape(2, 4, 4, 4, 2), ("tm_0", "tm_1", "space_0", "space_1", "space_2")
    )
    return jax.shard_map(
        per_device,
        mesh=split,
        in_specs=(
            P(TM_SPACE, None),
            P(),
            P(TM, None, None, SPACE),
            P(TM, SPACE),
            P(TM, SPACE),
            P(TM, SPACE),
            P(TM, SPACE),
        ),
        out_specs=(P(TM_SPACE, None), P()),
        check_vma=False,
    )
```

```python
import functools

import jax
import jax.numpy as jnp
import ml_dtypes
import numpy as np
from jax import lax
from jax.experimental import pallas as pl
from jax.experimental.pallas import tpu as pltpu
from jax.sharding import Mesh
from jax.sharding import PartitionSpec as P

PIECE = 1600
LEV = 4
BLOCKS = 13
ROWS = 64
OBS = 2048
CHUNK = 256
EARLY = 1280
VECTOR = (1,4,7,10,)


def split3(value):
    first = value.astype(jnp.bfloat16)
    rest = value - first.astype(jnp.float32)
    second = rest.astype(jnp.bfloat16)
    third = (rest - second.astype(jnp.float32)).astype(jnp.bfloat16)
    return first, second, third


def middle_kernel(early_ref, cases_hbm, f_ref, idx_ref, inn_ref, sig_ref, qc_ref, adj_ref, cost_ref,
                  late_ref, sums_by_lane, cells, table, modelled, grads, where_row, where_lane, sem):
    f32 = jnp.float32
    copy = pltpu.make_async_copy(cases_hbm.at[:, EARLY:, :], late_ref, sem)
    copy.start()
    cells[...] = jnp.zeros_like(cells)

    def forward(blk, start, width):
        if start < EARLY:
            rows = early_ref[:, start:start + width, :].reshape(8 * width, 256)
        else:
            rows = late_ref[:, start - EARLY:start - EARLY + width, :].reshape(8 * width, 256)
        if width == 128:
            fields = f_ref[:, blk * 32:(blk + 1) * 32, :].reshape(256, 128)
        else:
            tail = f_ref[:, 384:400, :].astype(f32)
            tail = jnp.concatenate([tail, pltpu.roll(tail, 64, axis=2)], axis=1)
            fields = tail.reshape(256, 128)[:, 0:64].astype(jnp.bfloat16)
        if blk in VECTOR:
            members = jnp.transpose(fields.astype(f32))
            for k in range(8):
                terms = rows[k * width:(k + 1) * width].astype(f32) * members
                at = k % LEV * BLOCKS + blk
                sums_by_lane[k // LEV, :, at:at + 1] = jnp.sum(terms, axis=1, keepdims=True)
            return
        prod = jnp.dot(rows, fields, preferred_element_type=f32)
        same = lax.broadcasted_iota(jnp.int32, (width, width), 0) == lax.broadcasted_iota(
            jnp.int32, (width, width), 1)
        for k in range(8):
            one = jnp.where(same, prod[k * width:(k + 1) * width], 0.0)
            row = jnp.sum(one, axis=0, keepdims=True)
            at = k % LEV * BLOCKS + blk
            cells[k // LEV, at:at + 1, 0:width] = row

    for blk in range(BLOCKS):
        if blk * 128 == EARLY:
            copy.wait()
        forward(blk, blk * 128, min(128, PIECE - blk * 128))

    index = idx_ref[...]
    level = ((index >= PIECE).astype(jnp.int32) + (index >= 2 * PIECE).astype(jnp.int32)
             + (index >= 3 * PIECE).astype(jnp.int32))
    point = index - level * PIECE
    where_row[...] = level * BLOCKS + (point >> 7)
    where_lane[...] = point & 127

    for t in range(2):
        column = lax.broadcasted_iota(jnp.int32, (128, ROWS), 1)
        summed = functools.reduce(jnp.logical_or, [
            column == level * BLOCKS + blk for level in range(LEV) for blk in VECTOR])
        parts = split3(jnp.where(summed, sums_by_lane[t], jnp.transpose(cells[t])))
        for k in range(3):
            table[t, :, k * ROWS:(k + 1) * ROWS] = parts[k]

    row_id = lax.broadcasted_iota(jnp.int32, (ROWS, CHUNK), 0)
    lane_id = lax.broadcasted_iota(jnp.int32, (128, CHUNK), 0)

    for t in range(2):
        for c in range(OBS // CHUNK):
            at = slice(c * CHUNK, (c + 1) * CHUNK)
            hot = jnp.where(row_id == where_row[t:t + 1, at], 1.0, 0.0).astype(jnp.bfloat16)
            hot = jnp.concatenate([hot, hot, hot], axis=0)
            lines = jnp.dot(table[t], hot, preferred_element_type=f32)
            lines = jnp.where(lane_id == where_lane[t:t + 1, at], lines, 0.0)
            modelled[t:t + 1, at] = jnp.sum(lines, axis=0, keepdims=True)

    sigma = sig_ref[...]
    kind = qc_ref[...]
    radius_sq = jnp.where(kind == 0, 16.0, jnp.where(kind == 1, 4.0, 1.0))
    scaled = (modelled[...] - inn_ref[...]) / sigma
    scaled_sq = scaled * scaled / radius_sq
    terms = 0.5 * radius_sq * jnp.log1p(scaled_sq)
    cost_ref[...] = jnp.broadcast_to(jnp.sum(terms, axis=(0, 1), keepdims=True), (8, 128))
    grad = scaled / ((1.0 + scaled_sq) * sigma)
    first, second, third = split3(grad)
    grads[0] = first.astype(f32)
    grads[1] = second.astype(f32)
    grads[2] = third.astype(f32)

    sums = []
    for t in range(2):
        total = jnp.zeros((3 * ROWS, 128), f32)
        for c in range(OBS // CHUNK):
            at = slice(c * CHUNK, (c + 1) * CHUNK)
            hot = row_id == where_row[t:t + 1, at]
            left = jnp.concatenate(
                [jnp.where(hot, grads[k, t:t + 1, at], 0.0).astype(jnp.bfloat16) for k in range(3)],
                axis=0)
            right = jnp.where(lane_id == where_lane[t:t + 1, at], 1.0, 0.0).astype(jnp.bfloat16)
            total = total + lax.dot_general(left, right, (((1,), (1,)), ((), ())),
                                            preferred_element_type=f32)
        sums.append(total[0:ROWS] + total[ROWS:2 * ROWS] + total[2 * ROWS:3 * ROWS])
    update = jnp.concatenate(sums, axis=0).astype(jnp.bfloat16).astype(f32)
    columns = jnp.transpose(update)
    same = lax.broadcasted_iota(jnp.int32, (128, 128), 0) == lax.broadcasted_iota(
        jnp.int32, (128, 128), 1)

    for blk in range(BLOCKS):
        start = blk * 128
        width = min(128, PIECE - start)
        held, first = (early_ref, start) if start < EARLY else (late_ref, start - EARLY)
        if blk % 3 != 0 and width == 128:
            diagonals = []
            for k in range(8):
                j = k // LEV * ROWS + k % LEV * BLOCKS + blk
                diagonals.append(jnp.where(same, update[j:j + 1], 0.0).astype(jnp.bfloat16))
            total = jnp.dot(jnp.concatenate(diagonals, axis=1),
                            held[:, first:first + width, :].reshape(8 * width, 256),
                            preferred_element_type=f32)
        else:
            cols = pltpu.roll(columns, (128 - blk) % 128, axis=1)
            halves = []
            for half in range(width // 64):
                lanes = slice(half * 64, half * 64 + 64)
                here = first + half * 64
                total = jnp.zeros((64, 256), f32)
                for k in range(8):
                    j = k // LEV * ROWS + k % LEV * BLOCKS
                    total = total + held[k, here:here + 64, :].astype(f32) * cols[lanes, j:j + 1]
                halves.append(total)
            total = jnp.concatenate(halves, axis=0)
        total = jnp.transpose(total)
        if width == 128:
            adj_ref[:, blk * 32:(blk + 1) * 32, :] = total.astype(jnp.bfloat16).reshape(8, 32, 128)
        else:
            total = total.reshape(8, 32, 64)
            total = jnp.concatenate([total[:, 0:16], total[:, 16:32]], axis=2)
            adj_ref[:, 384:400, :] = total.astype(jnp.bfloat16)


def middle(early, cases, fields, obs_index, innovation, obs_sigma, qc_class):
    vm = pl.BlockSpec(memory_space=pltpu.VMEM)
    return pl.pallas_call(
        middle_kernel,
        out_shape=(jax.ShapeDtypeStruct((8, 400, 128), jnp.bfloat16),
                   jax.ShapeDtypeStruct((8, 128), jnp.float32)),
        in_specs=[vm, pl.BlockSpec(memory_space=pltpu.HBM)] + [vm] * 5,
        out_specs=(vm, vm),
        scratch_shapes=[
            pltpu.VMEM((8, PIECE - EARLY, 256), jnp.bfloat16),
            pltpu.VMEM((2, 128, ROWS), jnp.float32),
            pltpu.VMEM((2, ROWS, 128), jnp.float32),
            pltpu.VMEM((2, 128, 3 * ROWS), jnp.bfloat16),
            pltpu.VMEM((2, OBS), jnp.float32),
            pltpu.VMEM((3, 2, OBS), jnp.float32),
            pltpu.VMEM((2, OBS), jnp.int32),
            pltpu.VMEM((2, OBS), jnp.int32),
            pltpu.SemaphoreType.DMA,
        ],
        compiler_params=pltpu.CompilerParams(vmem_limit_bytes=40 * 1024 * 1024),
        name="middle",
    )(early, pltpu.with_memory_space_constraint(cases, pltpu.HBM), fields, obs_index, innovation,
      obs_sigma, qc_class)


F32 = jnp.float32
BF16 = jnp.bfloat16
GX = 320
GY = 160
MEMBERS = 256
WIDE = 16 * 128
SPACE = ("space_0", "space_1", "space_2")
TM = ("tm_0", "tm_1")
TM_SPACE = ("tm_0", "tm_1", "space_0", "space_1", "space_2")


def two_parts(value):
    high = np.asarray(value, np.float32).astype(ml_dtypes.bfloat16)
    low = (value - high.astype(np.float64)).astype(np.float32).astype(ml_dtypes.bfloat16)
    return high, low


def lookup_table(length):
    wave = np.arange(length)[:, None]
    angle = np.pi * (np.arange(length)[None, :] + 0.5) * wave / length
    return np.cos(angle) * np.sqrt(np.where(wave == 0, 1.0, 2.0) / length)


def split2(value):
    high = value.astype(BF16)
    return high, (value - high.astype(F32)).astype(BF16)


def product(left, right):
    (left_high, left_low), (right_high, right_low) = left, right
    return (jnp.dot(left_high, right_high, preferred_element_type=F32)
            + (jnp.dot(left_low, right_high, preferred_element_type=F32)
               + jnp.dot(left_high, right_low, preferred_element_type=F32)))


def rows_of(flat, lines, grid):
    for k in range(5):
        lines[:, k * 128:(k + 1) * 128] = flat[pl.ds(k, 80, stride=5), :]
    for k in range(4):
        grid[k * 80:(k + 1) * 80, :] = lines[:, k * GY:(k + 1) * GY]


def flat_of(grid, lines, flat):
    for k in range(4):
        lines[:, k * GY:(k + 1) * GY] = grid[k * 80:(k + 1) * 80, :]
    for k in range(5):
        flat[pl.ds(k, 80, stride=5), :] = lines[:, k * 128:(k + 1) * 128]


def first_kernel(c_hbm, s_hbm, x_hbm, y_hbm, cases_hbm, out_ref, back_ref, early_ref,
                 wide, tall, lines, grid, c_ref, s_ref, x_ref, y_ref, sems):
    pairs = ((c_hbm, c_ref), (s_hbm, s_ref), (y_hbm, y_ref), (x_hbm, x_ref), (cases_hbm.at[:, 0:EARLY, :], early_ref))
    copies = [pltpu.make_async_copy(*pair, sems.at[k]) for k, pair in enumerate(pairs)]
    for copy in copies:
        copy.start()
    wide[:, PIECE:] = jnp.zeros((32, wide.shape[1] - PIECE), F32)
    copies[0].wait()
    control = c_ref[...]
    back = 0.5 * jnp.sum(control * control, axis=(0, 1), keepdims=True)
    back_ref[...] = jnp.broadcast_to(back, (8, 128))
    copies[1].wait()
    c_ref[...] = control * s_ref[...]
    rows_of(c_ref, lines, grid)
    coeffs = split2(grid[...])
    copies[2].wait()
    rows = split2(product(coeffs, (y_ref[0], y_ref[1])))
    copies[3].wait()
    field = product((x_ref[0], x_ref[1]), rows)
    for i in range(10):
        wide[:, i * GY:(i + 1) * GY] = field[i * 32:(i + 1) * 32]
    for r in range(BLOCKS):
        tall[:, r, :] = wide[:, r * 128:(r + 1) * 128]
    for r in range(BLOCKS, 16):
        tall[:, r, :] = jnp.zeros((32, 128), F32)
    out_ref[...] = tall[...].astype(BF16)
    copies[4].wait()


def spread_kernel(in_ref, out_ref, tall, lines):
    tall[...] = in_ref[...].astype(F32)
    for r in range(12):
        lines[r * 32:(r + 1) * 32, :] = tall[:, r, :]
    tail = tall[:, 12, :]
    lane = lax.broadcasted_iota(jnp.int32, (16, 128), 1)
    lines[384:400, :] = jnp.where(lane < 64, tail[0:16], pltpu.roll(tail[16:32], 64, axis=1))
    value = lines[...].astype(BF16)
    for k in range(8):
        out_ref[k] = value


def fold_kernel(in_ref, out_ref, tall):
    total = in_ref[0].astype(F32)
    for k in range(1, 8):
        total = total + in_ref[k].astype(F32)
    for r in range(12):
        tall[:, r, :] = total[r * 32:(r + 1) * 32]
    tail = total[384:400]
    tall[:, 12, :] = jnp.concatenate([tail, pltpu.roll(tail, 64, axis=1)], axis=0)
    for r in range(BLOCKS, 16):
        tall[:, r, :] = jnp.zeros((32, 128), F32)
    out_ref[...] = tall[...].astype(BF16)


def last_kernel(in_ref, c_ref, s_ref, xh, xl, yh, yl, back_ref, obs_ref, grad_ref, pay_ref,
                tall, wide, adj, lines, grid):
    tall[...] = in_ref[...].astype(F32)
    for r in range(BLOCKS):
        wide[:, r * 128:(r + 1) * 128] = tall[:, r, :]
    for i in range(10):
        adj[i * 32:(i + 1) * 32, :] = wide[:, i * GY:(i + 1) * GY].astype(BF16)
    part = adj[...]
    rows = (jnp.dot(xh[...], part, preferred_element_type=F32)
            + jnp.dot(xl[...], part, preferred_element_type=F32))
    grid[...] = product(split2(rows), (yh[...], yl[...]))
    flat_of(grid, lines, grad_ref)
    grad = c_ref[...] + s_ref[...] * grad_ref[...]
    grad_ref[...] = grad
    cost = back_ref[0:1, 0:1] + obs_ref[0:1, 0:1]
    norm = jnp.sum(grad * grad, axis=(0, 1), keepdims=True)
    lane = lax.broadcasted_iota(jnp.int32, (MEMBERS, 128), 1)
    pay_ref[...] = jnp.where(lane == 0, cost, jnp.where(lane == 1, norm, 0.0))


def step_kernel(pay_ref, c_ref, g_ref, out_ref, cost_ref):
    sums = jnp.sum(pay_ref[...], axis=0, keepdims=True)
    cost = sums[:, 0:1]
    size = 0.5 * cost / (sums[:, 1:2] + 1e-06)
    out_ref[...] = c_ref[...] - size * g_ref[...]
    cost_ref[...] = cost


def call(kernel, outs, scratch, name, specs=None):
    vm = pl.BlockSpec(memory_space=pltpu.VMEM)

    def run(*args):
        ins = [vm] * len(args)
        for at in specs or ():
            ins[at] = pl.BlockSpec(memory_space=pltpu.HBM)
        return pl.pallas_call(
            kernel,
            out_shape=tuple(jax.ShapeDtypeStruct(*out) for out in outs),
            in_specs=ins,
            out_specs=(vm,) * len(outs),
            scratch_shapes=scratch,
            compiler_params=pltpu.CompilerParams(vmem_limit_bytes=40 * 1024 * 1024),
            name=name,
        )(*args)

    return run


def exchanged(value, axis):
    return lax.all_to_all(value, axis, split_axis=0, concat_axis=0, tiled=True)


def per_device(control, spectrum, perturb, obs_index, innovation, obs_sigma, qc_class):
    waves = np.arange(GX).reshape(80, 4).T.reshape(-1)
    points = np.arange(GX).reshape(32, 10).T.reshape(-1)
    table_x = lookup_table(GX)[waves][:, points]
    table_y = lookup_table(GY)
    cases = perturb.transpose(0, 2, 3, 1).reshape(2 * LEV, PIECE, MEMBERS)
    control_flat = control.reshape(400, 128)
    spectrum_flat = spectrum.reshape(400, 128)
    tall = pltpu.VMEM((32, 16, 128), F32)
    wide = pltpu.VMEM((32, BLOCKS * 128), F32)
    lines = pltpu.VMEM((80, 640), F32)
    grid = pltpu.VMEM((GX, GY), F32)
    flat = pltpu.VMEM((400, 128), F32)

    inputs = (control_flat, spectrum_flat, jnp.asarray(np.stack(two_parts(table_x.T))),
              jnp.asarray(np.stack(two_parts(table_y))), cases)
    sent, back, early = call(
        first_kernel,
        (((32, 16, 128), BF16), ((8, 128), F32), ((2 * LEV, EARLY, MEMBERS), BF16)),
        [wide, tall, lines, grid, flat, flat, pltpu.VMEM((2, GX, GX), BF16),
         pltpu.VMEM((2, GY, GY), BF16), pltpu.SemaphoreType.DMA((5,))],
        "synthesis", specs=range(5),
    )(*[pltpu.with_memory_space_constraint(value, pltpu.HBM) for value in inputs])
    pieces = exchanged(sent, SPACE)
    (copies,) = call(spread_kernel, (((8, 400, 128), BF16),), [tall, flat], "spread")(pieces)
    fields = exchanged(copies, TM)
    partial, obs = middle(early, cases, fields, obs_index, innovation, obs_sigma, qc_class)
    terms = exchanged(partial, TM)
    (summed,) = call(fold_kernel, (((32, 16, 128), BF16),), [tall], "fold")(terms)
    adjoint = exchanged(summed, SPACE)
    gradient, mine = call(
        last_kernel,
        (((400, 128), F32), ((MEMBERS, 128), F32)),
        [tall, wide, pltpu.VMEM((GX, GY), BF16), lines, grid],
        "analysis",
    )(adjoint, control_flat, spectrum_flat, *two_parts(table_x), *two_parts(table_y.T), back, obs)
    sums = exchanged(mine.reshape(MEMBERS, 1, 128), TM_SPACE).reshape(MEMBERS, 128)
    result, cost = call(
        step_kernel, (((400, 128), F32), ((1, 1), F32)), [], "step"
    )(sums, control_flat, gradient)
    return result.reshape(1, GX * GY), cost.reshape(1)


def solution(mesh):
    split = Mesh(
        mesh.devices.reshape(2, 4, 4, 4, 2), ("tm_0", "tm_1", "space_0", "space_1", "space_2")
    )
    return jax.shard_map(
        per_device,
        mesh=split,
        in_specs=(
            P(TM_SPACE, None),
            P(),
            P(TM, None, None, SPACE),
            P(TM, SPACE),
            P(TM, SPACE),
            P(TM, SPACE),
            P(TM, SPACE),
        ),
        out_specs=(P(TM_SPACE, None), P()),
        check_vma=False,
    )
```

```python
import functools

import jax
import jax.numpy as jnp
import ml_dtypes
import numpy as np
from jax import lax
from jax.experimental import pallas as pl
from jax.experimental.pallas import tpu as pltpu
from jax.sharding import Mesh
from jax.sharding import PartitionSpec as P

PIECE = 1600
LEV = 4
BLOCKS = 13
ROWS = 64
OBS = 2048
CHUNK = 256
EARLY = 1280
VECTOR = (1,4,7,10,)


def split3(value):
    first = value.astype(jnp.bfloat16)
    rest = value - first.astype(jnp.float32)
    second = rest.astype(jnp.bfloat16)
    third = (rest - second.astype(jnp.float32)).astype(jnp.bfloat16)
    return first, second, third


def level_of(index):
    return ((index >= PIECE).astype(jnp.int32) + (index >= 2 * PIECE).astype(jnp.int32)
            + (index >= 3 * PIECE).astype(jnp.int32))


def middle_kernel(early_ref, cases_hbm, f_ref, row_hot, lane_hot, idx_ref, inn_ref, sig_ref, qc_ref, adj_ref, cost_ref,
                  late_ref, sums_by_lane, cells, table, modelled, grads, where_lane, sem):
    f32 = jnp.float32
    copy = pltpu.make_async_copy(cases_hbm.at[:, EARLY:, :], late_ref, sem)
    copy.start()
    cells[...] = jnp.zeros_like(cells)

    def forward(blk, start, width):
        if start < EARLY:
            rows = early_ref[:, start:start + width, :].reshape(8 * width, 256)
        else:
            rows = late_ref[:, start - EARLY:start - EARLY + width, :].reshape(8 * width, 256)
        if width == 128:
            fields = f_ref[:, blk * 32:(blk + 1) * 32, :].reshape(256, 128)
        else:
            tail = f_ref[:, 384:400, :].astype(f32)
            tail = jnp.concatenate([tail, pltpu.roll(tail, 64, axis=2)], axis=1)
            fields = tail.reshape(256, 128)[:, 0:64].astype(jnp.bfloat16)
        if blk in VECTOR:
            members = jnp.transpose(fields.astype(f32))
            for k in range(8):
                terms = rows[k * width:(k + 1) * width].astype(f32) * members
                at = k % LEV * BLOCKS + blk
                sums_by_lane[k // LEV, :, at:at + 1] = jnp.sum(terms, axis=1, keepdims=True)
            return
        prod = jnp.dot(rows, fields, preferred_element_type=f32)
        same = lax.broadcasted_iota(jnp.int32, (width, width), 0) == lax.broadcasted_iota(
            jnp.int32, (width, width), 1)
        for k in range(8):
            one = jnp.where(same, prod[k * width:(k + 1) * width], 0.0)
            row = jnp.sum(one, axis=0, keepdims=True)
            at = k % LEV * BLOCKS + blk
            cells[k // LEV, at:at + 1, 0:width] = row

    for blk in range(BLOCKS):
        if blk * 128 == EARLY:
            copy.wait()
        forward(blk, blk * 128, min(128, PIECE - blk * 128))

    index = idx_ref[...]
    where_lane[...] = (index - level_of(index) * PIECE) & 127

    for t in range(2):
        column = lax.broadcasted_iota(jnp.int32, (128, ROWS), 1)
        summed = functools.reduce(jnp.logical_or, [
            column == level * BLOCKS + blk for level in range(LEV) for blk in VECTOR])
        parts = split3(jnp.where(summed, sums_by_lane[t], jnp.transpose(cells[t])))
        for k in range(3):
            table[t, :, k * ROWS:(k + 1) * ROWS] = parts[k]

    lane_id = lax.broadcasted_iota(jnp.int32, (128, CHUNK), 0)

    for t in range(2):
        for c in range(OBS // CHUNK):
            at = slice(c * CHUNK, (c + 1) * CHUNK)
            hot = row_hot[t, :, at]
            hot = jnp.concatenate([hot, hot, hot], axis=0)
            lines = jnp.dot(table[t], hot, preferred_element_type=f32)
            lines = jnp.where(lane_id == where_lane[t:t + 1, at], lines, 0.0)
            modelled[t:t + 1, at] = jnp.sum(lines, axis=0, keepdims=True)

    sigma = sig_ref[...]
    kind = qc_ref[...]
    radius_sq = jnp.where(kind == 0, 16.0, jnp.where(kind == 1, 4.0, 1.0))
    scaled = (modelled[...] - inn_ref[...]) / sigma
    scaled_sq = scaled * scaled / radius_sq
    terms = 0.5 * radius_sq * jnp.log1p(scaled_sq)
    cost_ref[...] = jnp.broadcast_to(jnp.sum(terms, axis=(0, 1), keepdims=True), (8, 128))
    grad = scaled / ((1.0 + scaled_sq) * sigma)
    first, second, third = split3(grad)
    grads[0] = first.astype(f32)
    grads[1] = second.astype(f32)
    grads[2] = third.astype(f32)

    sums = []
    for t in range(2):
        total = jnp.zeros((3 * ROWS, 128), f32)
        for c in range(OBS // CHUNK):
            at = slice(c * CHUNK, (c + 1) * CHUNK)
            hot = row_hot[t, :, at]
            left = jnp.concatenate(
                [hot * grads[k, t:t + 1, at].astype(jnp.bfloat16) for k in range(3)], axis=0)
            right = lane_hot[t, :, at]
            total = total + lax.dot_general(left, right, (((1,), (1,)), ((), ())),
                                            preferred_element_type=f32)
        sums.append(total[0:ROWS] + total[ROWS:2 * ROWS] + total[2 * ROWS:3 * ROWS])
    update = jnp.concatenate(sums, axis=0).astype(jnp.bfloat16).astype(f32)
    columns = jnp.transpose(update)
    same = lax.broadcasted_iota(jnp.int32, (128, 128), 0) == lax.broadcasted_iota(
        jnp.int32, (128, 128), 1)

    for blk in range(BLOCKS):
        start = blk * 128
        width = min(128, PIECE - start)
        held, first = (early_ref, start) if start < EARLY else (late_ref, start - EARLY)
        if blk % 3 != 0 and width == 128:
            diagonals = []
            for k in range(8):
                j = k // LEV * ROWS + k % LEV * BLOCKS + blk
                diagonals.append(jnp.where(same, update[j:j + 1], 0.0).astype(jnp.bfloat16))
            total = jnp.dot(jnp.concatenate(diagonals, axis=1),
                            held[:, first:first + width, :].reshape(8 * width, 256),
                            preferred_element_type=f32)
        else:
            cols = pltpu.roll(columns, (128 - blk) % 128, axis=1)
            halves = []
            for half in range(width // 64):
                lanes = slice(half * 64, half * 64 + 64)
                here = first + half * 64
                total = jnp.zeros((64, 256), f32)
                for k in range(8):
                    j = k // LEV * ROWS + k % LEV * BLOCKS
                    total = total + held[k, here:here + 64, :].astype(f32) * cols[lanes, j:j + 1]
                halves.append(total)
            total = jnp.concatenate(halves, axis=0)
        total = jnp.transpose(total)
        if width == 128:
            adj_ref[:, blk * 32:(blk + 1) * 32, :] = total.astype(jnp.bfloat16).reshape(8, 32, 128)
        else:
            total = total.reshape(8, 32, 64)
            total = jnp.concatenate([total[:, 0:16], total[:, 16:32]], axis=2)
            adj_ref[:, 384:400, :] = total.astype(jnp.bfloat16)


def middle(early, cases, fields, row_hot, lane_hot, obs_index, innovation, obs_sigma, qc_class):
    vm = pl.BlockSpec(memory_space=pltpu.VMEM)
    return pl.pallas_call(
        middle_kernel,
        out_shape=(jax.ShapeDtypeStruct((8, 400, 128), jnp.bfloat16),
                   jax.ShapeDtypeStruct((8, 128), jnp.float32)),
        in_specs=[vm, pl.BlockSpec(memory_space=pltpu.HBM)] + [vm] * 7,
        out_specs=(vm, vm),
        scratch_shapes=[
            pltpu.VMEM((8, PIECE - EARLY, 256), jnp.bfloat16),
            pltpu.VMEM((2, 128, ROWS), jnp.float32),
            pltpu.VMEM((2, ROWS, 128), jnp.float32),
            pltpu.VMEM((2, 128, 3 * ROWS), jnp.bfloat16),
            pltpu.VMEM((2, OBS), jnp.float32),
            pltpu.VMEM((3, 2, OBS), jnp.float32),
            pltpu.VMEM((2, OBS), jnp.int32),
            pltpu.SemaphoreType.DMA,
        ],
        compiler_params=pltpu.CompilerParams(vmem_limit_bytes=40 * 1024 * 1024),
        name="middle",
    )(early, pltpu.with_memory_space_constraint(cases, pltpu.HBM), fields, row_hot, lane_hot, obs_index, innovation,
      obs_sigma, qc_class)


F32 = jnp.float32
BF16 = jnp.bfloat16
GX = 320
GY = 160
MEMBERS = 256
WIDE = 16 * 128
SPACE = ("space_0", "space_1", "space_2")
TM = ("tm_0", "tm_1")
TM_SPACE = ("tm_0", "tm_1", "space_0", "space_1", "space_2")


def two_parts(value):
    high = np.asarray(value, np.float32).astype(ml_dtypes.bfloat16)
    low = (value - high.astype(np.float64)).astype(np.float32).astype(ml_dtypes.bfloat16)
    return high, low


def lookup_table(length):
    wave = np.arange(length)[:, None]
    angle = np.pi * (np.arange(length)[None, :] + 0.5) * wave / length
    return np.cos(angle) * np.sqrt(np.where(wave == 0, 1.0, 2.0) / length)


def split2(value):
    high = value.astype(BF16)
    return high, (value - high.astype(F32)).astype(BF16)


def product(left, right):
    (left_high, left_low), (right_high, right_low) = left, right
    return (jnp.dot(left_high, right_high, preferred_element_type=F32)
            + (jnp.dot(left_low, right_high, preferred_element_type=F32)
               + jnp.dot(left_high, right_low, preferred_element_type=F32)))


def rows_of(flat, lines, grid):
    for k in range(5):
        lines[:, k * 128:(k + 1) * 128] = flat[pl.ds(k, 80, stride=5), :]
    for k in range(4):
        grid[k * 80:(k + 1) * 80, :] = lines[:, k * GY:(k + 1) * GY]


def flat_of(grid, lines, flat):
    for k in range(4):
        lines[:, k * GY:(k + 1) * GY] = grid[k * 80:(k + 1) * 80, :]
    for k in range(5):
        flat[pl.ds(k, 80, stride=5), :] = lines[:, k * 128:(k + 1) * 128]


def first_kernel(c_hbm, s_hbm, x_hbm, y_hbm, cases_hbm, idx_hbm, out_ref, back_ref, early_ref, row_hot, lane_hot,
                 wide, tall, lines, grid, c_ref, s_ref, x_ref, y_ref, idx_ref, sems):
    pairs = ((c_hbm, c_ref), (s_hbm, s_ref), (y_hbm, y_ref), (x_hbm, x_ref), (idx_hbm, idx_ref),
             (cases_hbm.at[:, 0:EARLY, :], early_ref))
    copies = [pltpu.make_async_copy(*pair, sems.at[k]) for k, pair in enumerate(pairs)]
    for copy in copies:
        copy.start()
    wide[:, PIECE:] = jnp.zeros((32, wide.shape[1] - PIECE), F32)
    copies[0].wait()
    control = c_ref[...]
    back = 0.5 * jnp.sum(control * control, axis=(0, 1), keepdims=True)
    back_ref[...] = jnp.broadcast_to(back, (8, 128))
    copies[1].wait()
    c_ref[...] = control * s_ref[...]
    rows_of(c_ref, lines, grid)
    coeffs = split2(grid[...])
    copies[2].wait()
    rows = split2(product(coeffs, (y_ref[0], y_ref[1])))
    copies[3].wait()
    field = product((x_ref[0], x_ref[1]), rows)
    for i in range(10):
        wide[:, i * GY:(i + 1) * GY] = field[i * 32:(i + 1) * 32]
    for r in range(BLOCKS):
        tall[:, r, :] = wide[:, r * 128:(r + 1) * 128]
    for r in range(BLOCKS, 16):
        tall[:, r, :] = jnp.zeros((32, 128), F32)
    out_ref[...] = tall[...].astype(BF16)
    copies[4].wait()
    index = idx_ref[...]
    level = level_of(index)
    point = index - level * PIECE
    row = level * BLOCKS + (point >> 7)
    lane = point & 127
    row_id = lax.broadcasted_iota(jnp.int32, (ROWS, OBS), 0)
    lane_id = lax.broadcasted_iota(jnp.int32, (128, OBS), 0)
    for t in range(2):
        row_hot[t] = jnp.where(row_id == row[t:t + 1], 1.0, 0.0).astype(BF16)
        lane_hot[t] = jnp.where(lane_id == lane[t:t + 1], 1.0, 0.0).astype(BF16)
    copies[5].wait()


def spread_kernel(in_ref, out_ref, tall, lines):
    tall[...] = in_ref[...].astype(F32)
    for r in range(12):
        lines[r * 32:(r + 1) * 32, :] = tall[:, r, :]
    tail = tall[:, 12, :]
    lane = lax.broadcasted_iota(jnp.int32, (16, 128), 1)
    lines[384:400, :] = jnp.where(lane < 64, tail[0:16], pltpu.roll(tail[16:32], 64, axis=1))
    value = lines[...].astype(BF16)
    for k in range(8):
        out_ref[k] = value


def fold_kernel(in_ref, out_ref, tall):
    total = in_ref[0].astype(F32)
    for k in range(1, 8):
        total = total + in_ref[k].astype(F32)
    for r in range(12):
        tall[:, r, :] = total[r * 32:(r + 1) * 32]
    tail = total[384:400]
    tall[:, 12, :] = jnp.concatenate([tail, pltpu.roll(tail, 64, axis=1)], axis=0)
    for r in range(BLOCKS, 16):
        tall[:, r, :] = jnp.zeros((32, 128), F32)
    out_ref[...] = tall[...].astype(BF16)


def last_kernel(in_ref, c_ref, s_ref, xh, xl, yh, yl, back_ref, obs_ref, grad_ref, pay_ref,
                tall, wide, adj, lines, grid):
    tall[...] = in_ref[...].astype(F32)
    for r in range(BLOCKS):
        wide[:, r * 128:(r + 1) * 128] = tall[:, r, :]
    for i in range(10):
        adj[i * 32:(i + 1) * 32, :] = wide[:, i * GY:(i + 1) * GY].astype(BF16)
    part = adj[...]
    rows = (jnp.dot(xh[...], part, preferred_element_type=F32)
            + jnp.dot(xl[...], part, preferred_element_type=F32))
    grid[...] = product(split2(rows), (yh[...], yl[...]))
    flat_of(grid, lines, grad_ref)
    grad = c_ref[...] + s_ref[...] * grad_ref[...]
    grad_ref[...] = grad
    cost = back_ref[0:1, 0:1] + obs_ref[0:1, 0:1]
    norm = jnp.sum(grad * grad, axis=(0, 1), keepdims=True)
    lane = lax.broadcasted_iota(jnp.int32, (MEMBERS, 128), 1)
    pay_ref[...] = jnp.where(lane == 0, cost, jnp.where(lane == 1, norm, 0.0))


def step_kernel(pay_ref, c_ref, g_ref, out_ref, cost_ref):
    sums = jnp.sum(pay_ref[...], axis=0, keepdims=True)
    cost = sums[:, 0:1]
    size = 0.5 * cost / (sums[:, 1:2] + 1e-06)
    out_ref[...] = c_ref[...] - size * g_ref[...]
    cost_ref[...] = cost


def call(kernel, outs, scratch, name, specs=None):
    vm = pl.BlockSpec(memory_space=pltpu.VMEM)

    def run(*args):
        ins = [vm] * len(args)
        for at in specs or ():
            ins[at] = pl.BlockSpec(memory_space=pltpu.HBM)
        return pl.pallas_call(
            kernel,
            out_shape=tuple(jax.ShapeDtypeStruct(*out) for out in outs),
            in_specs=ins,
            out_specs=(vm,) * len(outs),
            scratch_shapes=scratch,
            compiler_params=pltpu.CompilerParams(vmem_limit_bytes=40 * 1024 * 1024),
            name=name,
        )(*args)

    return run


def exchanged(value, axis):
    return lax.all_to_all(value, axis, split_axis=0, concat_axis=0, tiled=True)


def per_device(control, spectrum, perturb, obs_index, innovation, obs_sigma, qc_class):
    waves = np.arange(GX).reshape(80, 4).T.reshape(-1)
    points = np.arange(GX).reshape(32, 10).T.reshape(-1)
    table_x = lookup_table(GX)[waves][:, points]
    table_y = lookup_table(GY)
    cases = perturb.transpose(0, 2, 3, 1).reshape(2 * LEV, PIECE, MEMBERS)
    control_flat = control.reshape(400, 128)
    spectrum_flat = spectrum.reshape(400, 128)
    tall = pltpu.VMEM((32, 16, 128), F32)
    wide = pltpu.VMEM((32, BLOCKS * 128), F32)
    lines = pltpu.VMEM((80, 640), F32)
    grid = pltpu.VMEM((GX, GY), F32)
    flat = pltpu.VMEM((400, 128), F32)

    inputs = (control_flat, spectrum_flat, jnp.asarray(np.stack(two_parts(table_x.T))),
              jnp.asarray(np.stack(two_parts(table_y))), cases, obs_index)
    sent, back, early, row_hot, lane_hot = call(
        first_kernel,
        (((32, 16, 128), BF16), ((8, 128), F32), ((2 * LEV, EARLY, MEMBERS), BF16),
         ((2, ROWS, OBS), BF16), ((2, 128, OBS), BF16)),
        [wide, tall, lines, grid, flat, flat, pltpu.VMEM((2, GX, GX), BF16),
         pltpu.VMEM((2, GY, GY), BF16), pltpu.VMEM((2, OBS), jnp.int32), pltpu.SemaphoreType.DMA((6,))],
        "synthesis", specs=range(6),
    )(*[pltpu.with_memory_space_constraint(value, pltpu.HBM) for value in inputs])
    pieces = exchanged(sent, SPACE)
    (copies,) = call(spread_kernel, (((8, 400, 128), BF16),), [tall, flat], "spread")(pieces)
    fields = exchanged(copies, TM)
    partial, obs = middle(early, cases, fields, row_hot, lane_hot, obs_index, innovation, obs_sigma, qc_class)
    terms = exchanged(partial, TM)
    (summed,) = call(fold_kernel, (((32, 16, 128), BF16),), [tall], "fold")(terms)
    adjoint = exchanged(summed, SPACE)
    gradient, mine = call(
        last_kernel,
        (((400, 128), F32), ((MEMBERS, 128), F32)),
        [tall, wide, pltpu.VMEM((GX, GY), BF16), lines, grid],
        "analysis",
    )(adjoint, control_flat, spectrum_flat, *two_parts(table_x), *two_parts(table_y.T), back, obs)
    sums = exchanged(mine.reshape(MEMBERS, 1, 128), TM_SPACE).reshape(MEMBERS, 128)
    result, cost = call(
        step_kernel, (((400, 128), F32), ((1, 1), F32)), [], "step"
    )(sums, control_flat, gradient)
    return result.reshape(1, GX * GY), cost.reshape(1)


def solution(mesh):
    split = Mesh(
        mesh.devices.reshape(2, 4, 4, 4, 2), ("tm_0", "tm_1", "space_0", "space_1", "space_2")
    )
    return jax.shard_map(
        per_device,
        mesh=split,
        in_specs=(
            P(TM_SPACE, None),
            P(),
            P(TM, None, None, SPACE),
            P(TM, SPACE),
            P(TM, SPACE),
            P(TM, SPACE),
            P(TM, SPACE),
        ),
        out_specs=(P(TM_SPACE, None), P()),
        check_vma=False,
    )
```
